32 devices in a mesh: section: 2 (over x), dp: 4 (over z), row: 2 (over y), col: 2 (over core).
Axes of the slice: x: 2, y: 2, z: 4, core: 2. Of those that a mesh axis runs over, the one named last changes fastest.
Arguments:
- latents_in: bfloat16 [4096, 384], P(('dp', 'row'), 'col'), may hold values from -4 to 4
- labels: int32 [16], P(('dp', 'row')), may hold values from 0 to 999
- timesteps: int32 [16], P(('dp', 'row')), may hold values from 0 to 999
- out_grad: bfloat16 [4096, 384], P(('dp', 'row'), 'col'), may hold values from -6 to 6
- label_table: bfloat16 [1000, 384], replicated, may hold values from -6 to 6
- time_table: bfloat16 [1000, 384], replicated, may hold values from -6 to 6
- ada_w: bfloat16 [2, 384, 6, 384], P('section', None, None, 'col'), may hold values from -0.3125 to 0.3125
- ada_b: float32 [2, 6, 384], P('section', None, 'col'), may hold values from -1.5 to 1.5
- qkv_w: bfloat16 [2, 384, 3, 384], P('section', 'col', None, 'row'), may hold values from -0.3125 to 0.3125
- qkv_b: float32 [2, 3, 384], P('section', None, 'row'), may hold values from -1.5 to 1.5
- proj_w: bfloat16 [2, 384, 384], P('section', 'row', 'col'), may hold values from -2.5 to 2.5
- proj_b: float32 [2, 384], P('section', 'col'), may hold values from -1.5 to 1.5
- fc1_w: bfloat16 [2, 384, 1536], P('section', 'col', 'row'), may hold values from -0.3125 to 0.3125
- fc1_b: float32 [2, 1536], P('section', 'row'), may hold values from -1.5 to 1.5
- fc2_w: bfloat16 [2, 1536, 384], P('section', 'row', 'col'), may hold values from -0.15625 to 0.15625
- fc2_b: float32 [2, 384], P('section', 'col'), may hold values from -1.5 to 1.5
Outputs:
- block_outs: bfloat16 [2, 4096, 384], P('section', ('dp', 'row'), 'col')
- input_grads: float32 [2, 4096, 384], P('section', ('dp', 'row'), 'col')
- cond_grad: float32 [16, 384], P(('dp', 'row'))
- label_table_grad: float32 [1000, 384], replicated
- time_table_grad: float32 [1000, 384], replicated
- ada_w_grad: float32 [2, 384, 6, 384], P('section', None, None, 'col')
- ada_b_grad: float32 [2, 6, 384], P('section', None, 'col')
- qkv_w_grad: float32 [2, 384, 3, 384], P('section', 'col', None, 'row')
- qkv_b_grad: float32 [2, 3, 384], P('section', None, 'row')
- proj_w_grad: float32 [2, 384, 384], P('section', 'row', 'col')
- proj_b_grad: float32 [2, 384], P('section', 'col')
- fc1_w_grad: float32 [2, 384, 1536], P('section', 'col', 'row')
- fc1_b_grad: float32 [2, 1536], P('section', 'row')
- fc2_w_grad: float32 [2, 1536, 384], P('section', 'row', 'col')
- fc2_b_grad: float32 [2, 384], P('section', 'col')
The draws below stay inside these ranges and needn't reach their ends.
All inputs are finite; a program needn't handle non-finite values.
Results may differ from the reference program's by a relative error of at most 0.035.
The reference program's roundings to bfloat16 on the way count: a program that leaves them out, or rounds other values in their place, can miss the bound.
Values may be sent and summed in bfloat16 or wider, within the bound.
A program may use at most 128 MiB of HBM per device.

```python
import jax
import jax.numpy as jnp
from jax import lax

D = 384
HEADS = 6
HD = 64
FF = 1536
SEQ = 256
CLASSES = 1000
STEPS = 1000
LATENTS = 16
TOKENS = 4096


def draw_latents_in(key, part):
    base = jax.random.truncated_normal(key, -4.0, 4.0, (TOKENS, D), jnp.float32)
    return base.astype(jnp.bfloat16)


def plant(drawn, rng, low, largest):
    extent = drawn.shape
    index_at = [jax.random.randint(jax.random.fold_in(rng, axis), (), 0, extent[axis]) for axis in range(len(extent))]
    drawn = drawn.at[tuple(index_at)].set(low)
    longest = extent.index(max(extent))
    index_at[longest] = (index_at[longest] + 1) % extent[longest]
    return drawn.at[tuple(index_at)].set(largest)


def levels(key, dims, pieces, smallest, top_value):
    factor_of, own = 1.0, jax.random.fold_in(key, 6)
    for dim, blocks in pieces:
        heights = jnp.exp(jax.random.uniform(jax.random.fold_in(own, dim), (blocks,), jnp.float32, smallest / len(pieces), top_value / len(pieces)))
        factor_of = factor_of * jnp.repeat(heights, dims[dim] // blocks).reshape([-1 if axis == dim else 1 for axis in range(len(dims))])
    return factor_of


def bell_draw(key, dims, scale, limit, cuts=(), dtype=jnp.bfloat16):
    values = jax.random.normal(key, dims, jnp.float32) * scale
    if len(cuts) > 0:
        values = levels(key, dims, cuts, -0.22, 0.18) * values
    return jnp.clip(values, min=-limit, max=limit).astype(dtype)


def setup_inputs(seed: int = 0) -> dict:
    seeds = jax.random.split(jax.random.key(seed), 17)
    latents_in = draw_latents_in(jax.random.fold_in(seeds[16], 71), 0)
    labels = plant(jax.random.randint(seeds[1], (LATENTS,), 0, CLASSES), jax.random.fold_in(seeds[1], 1), 0, CLASSES - 1).astype(jnp.int32)
    timesteps = plant(jax.random.randint(seeds[2], (LATENTS,), 0, STEPS), jax.random.fold_in(seeds[2], 1), 0, STEPS - 1).astype(jnp.int32)
    out_grad = bell_draw(seeds[3], (TOKENS, D), 1.0, 6.0, ((0, 8), (1, 2)))
    label_table = bell_draw(seeds[4], (CLASSES, D), 1.0, 6.0)
    time_table = bell_draw(seeds[5], (STEPS, D), 1.0, 6.0)
    ada_w = bell_draw(seeds[6], (2, D, 6, D), D ** -0.5, 0.3125, ((0, 2), (3, 2)))
    ada_b = bell_draw(seeds[7], (2, 6, D), 0.3, 1.5, ((0, 2), (2, 2)), jnp.float32)
    qkv_w = bell_draw(seeds[8], (2, D, 3, D), D ** -0.5, 0.3125, ((0, 2), (1, 2), (3, 2)))
    qkv_b = bell_draw(seeds[9], (2, 3, D), 0.3, 1.5, ((0, 2), (2, 2)), jnp.float32)
    proj_w = bell_draw(seeds[10], (2, D, D), (4 * D // SEQ) ** -0.5, 2.5, ((0, 2), (1, 2), (2, 2)))
    proj_b = bell_draw(seeds[11], (2, D), 0.3, 1.5, ((0, 2), (1, 2)), jnp.float32)
    fc1_w = bell_draw(seeds[12], (2, D, FF), D ** -0.5, 0.3125, ((0, 2), (1, 2), (2, 2)))
    fc1_b = bell_draw(seeds[13], (2, FF), 0.3, 1.5, ((0, 2), (1, 2)), jnp.float32)
    fc2_w = bell_draw(seeds[14], (2, FF, D), FF ** -0.5, 0.15625, ((0, 2), (1, 2), (2, 2)))
    fc2_b = bell_draw(seeds[15], (2, D), 0.3, 1.5, ((0, 2), (1, 2)), jnp.float32)
    return dict(latents_in=latents_in, labels=labels, timesteps=timesteps, out_grad=out_grad, label_table=label_table, time_table=time_table, ada_w=ada_w, ada_b=ada_b, qkv_w=qkv_w, qkv_b=qkv_b, proj_w=proj_w, proj_b=proj_b, fc1_w=fc1_w, fc1_b=fc1_b, fc2_w=fc2_w, fc2_b=fc2_b)


EPS = 1e-06

def rounded(value):
    return lax.optimization_barrier(value.astype(jnp.bfloat16))

def matmul(left_arr, right_arr):
    return jnp.dot(left_arr, right_arr, preferred_element_type=jnp.float32)

def norm_rows(stream):
    mean_val = lax.optimization_barrier(jnp.mean(stream, axis=-1, keepdims=True))
    variance = lax.optimization_barrier(jnp.mean(jnp.square(stream - mean_val), axis=-1, keepdims=True))
    inv_std = lax.rsqrt(variance + EPS)
    return ((stream - mean_val) * inv_std, inv_std)

def norm_back(grad_norm, normed, inv_std):
    return inv_std * (grad_norm - lax.optimization_barrier(jnp.mean(grad_norm, axis=-1, keepdims=True)) - normed * lax.optimization_barrier(jnp.mean(grad_norm * normed, axis=-1, keepdims=True)))

def gelu_back(pre_act, grad_act):
    return jax.vjp(lambda value: jax.nn.gelu(value, approximate=True), pre_act)[1](grad_act)[0]

def block_forward(stream, modul, params):
    w_qkv, b_qkv, w_proj, b_proj, w_up, b_up, w_down, b_down = params
    scale = 1.0 / HD ** 0.5
    normed1, inv1 = norm_rows(stream)
    hidden1 = (normed1 * (1.0 + modul[1]) + modul[0]).astype(jnp.bfloat16)
    packed = rounded(matmul(hidden1, w_qkv.reshape(D, 3 * D)) + b_qkv.reshape(3 * D))
    parts = packed.reshape(SEQ, 3, HEADS, HD).astype(jnp.float32)
    queries, keys_part, values = (parts[:, 0], parts[:, 1], parts[:, 2])
    scores = jnp.einsum('qhd,khd->hqk', queries, keys_part) * scale
    log_total = jax.nn.logsumexp(scores, axis=-1)
    prob_low = rounded(jnp.exp(scores - log_total[..., None])).astype(jnp.float32)
    attended = jnp.einsum('hqk,khd->qhd', prob_low, values).astype(jnp.bfloat16).reshape(SEQ, D)
    branch_a = matmul(attended, w_proj) + b_proj
    middle = stream + modul[2] * branch_a
    normed2, inv2 = norm_rows(middle)
    hidden2 = (normed2 * (1.0 + modul[4]) + modul[3]).astype(jnp.bfloat16)
    pre_act = matmul(hidden2, w_up) + b_up
    activ = jax.nn.gelu(pre_act, approximate=True).astype(jnp.bfloat16)
    branch_f = matmul(activ, w_down) + b_down
    result = middle + modul[5] * branch_f
    saved = (normed1, inv1, hidden1, packed, log_total, attended, branch_a, normed2, inv2, hidden2, pre_act, activ, branch_f)
    return (result, saved)

def block_backward(grad_out, modul, params, saved):
    w_qkv, b_qkv, w_proj, b_proj, w_up, b_up, w_down, b_down = params
    normed1, inv1, hidden1, packed, log_total, attended, branch_a, normed2, inv2, hidden2, pre_act, activ, branch_f = saved
    scale = 1.0 / HD ** 0.5
    d_gate2 = lax.optimization_barrier(jnp.sum(grad_out * branch_f, axis=0))
    grad_f = (grad_out * modul[5]).astype(jnp.bfloat16)
    g_down = matmul(activ.T, grad_f)
    g_bdown = lax.optimization_barrier(jnp.sum(grad_f.astype(jnp.float32), axis=0))
    grad_act = matmul(grad_f, w_down.T)
    grad_pre = gelu_back(pre_act, grad_act).astype(jnp.bfloat16)
    g_up = matmul(hidden2.T, grad_pre)
    g_bup = lax.optimization_barrier(jnp.sum(grad_pre.astype(jnp.float32), axis=0))
    grad_h2 = matmul(grad_pre, w_up.T)
    d_scale2 = lax.optimization_barrier(jnp.sum(grad_h2 * normed2, axis=0))
    d_shift2 = lax.optimization_barrier(jnp.sum(grad_h2, axis=0))
    grad_mid = grad_out + norm_back(grad_h2 * (1.0 + modul[4]), normed2, inv2)
    d_gate1 = lax.optimization_barrier(jnp.sum(grad_mid * branch_a, axis=0))
    grad_a = (grad_mid * modul[2]).astype(jnp.bfloat16)
    g_proj = matmul(attended.T, grad_a)
    g_bproj = lax.optimization_barrier(jnp.sum(grad_a.astype(jnp.float32), axis=0))
    grad_att = rounded(matmul(grad_a, w_proj.T)).astype(jnp.float32).reshape(SEQ, HEADS, HD)
    parts = packed.reshape(SEQ, 3, HEADS, HD).astype(jnp.float32)
    queries, keys_part, values = (parts[:, 0], parts[:, 1], parts[:, 2])
    scores = jnp.einsum('qhd,khd->hqk', queries, keys_part) * scale
    prob_full = jnp.exp(scores - log_total[..., None])
    prob_low = rounded(prob_full).astype(jnp.float32)
    grad_values = jnp.einsum('hqk,qhd->khd', prob_low, grad_att)
    grad_prob = jnp.einsum('qhd,khd->hqk', grad_att, values)
    delta = lax.optimization_barrier(jnp.sum(prob_full * grad_prob, axis=-1, keepdims=True))
    grad_scores = rounded(prob_full * (grad_prob - delta) * scale).astype(jnp.float32)
    grad_queries = jnp.einsum('hqk,khd->qhd', grad_scores, keys_part)
    grad_keys = jnp.einsum('hqk,qhd->khd', grad_scores, queries)
    grad_packed = jnp.stack([grad_queries, grad_keys, grad_values], axis=1).astype(jnp.bfloat16).reshape(SEQ, 3 * D)
    g_qkv = matmul(hidden1.T, grad_packed).reshape(D, 3, D)
    g_bqkv = lax.optimization_barrier(jnp.sum(grad_packed.astype(jnp.float32), axis=0)).reshape(3, D)
    grad_h1 = matmul(grad_packed, w_qkv.reshape(D, 3 * D).T)
    d_scale1 = lax.optimization_barrier(jnp.sum(grad_h1 * normed1, axis=0))
    d_shift1 = lax.optimization_barrier(jnp.sum(grad_h1, axis=0))
    grad_in = grad_mid + norm_back(grad_h1 * (1.0 + modul[1]), normed1, inv1)
    d_mod = jnp.stack([d_shift1, d_scale1, d_gate1, d_shift2, d_scale2, d_gate2])
    return (grad_in, (g_qkv, g_bqkv, g_proj, g_bproj, g_up, g_bup, g_down, g_bdown), d_mod)

def reference(latents_in, labels, timesteps, out_grad, label_table, time_table, ada_w, ada_b, qkv_w, qkv_b, proj_w, proj_b, fc1_w, fc1_b, fc2_w, fc2_b):
    stacks = (qkv_w, qkv_b, proj_w, proj_b, fc1_w, fc1_b, fc2_w, fc2_b)
    params = [tuple((arr[section_index] for arr in stacks)) for section_index in range(2)]
    ada_flat = [ada_w[section_index].reshape(D, 6 * D) for section_index in range(2)]
    zero_blocks = tuple((tuple((jnp.zeros(arr.shape[1:], jnp.float32) for arr in stacks)) for section_index in range(2)))
    zero_ada = tuple((jnp.zeros((D, 6 * D), jnp.float32) for section_index in range(2)))
    zero_adab = tuple((jnp.zeros((6, D), jnp.float32) for section_index in range(2)))
    carry_init = (zero_blocks, zero_ada, zero_adab, jnp.zeros((CLASSES, D), jnp.float32), jnp.zeros((STEPS, D), jnp.float32))

    def per_latent(carry, item):
        block_grads, ada_grads, adab_grads, label_grad, time_grad = carry
        tokens_in, cotangent, label_id, step_id = item
        cond = label_table[label_id].astype(jnp.float32) + time_table[step_id].astype(jnp.float32)
        silu_low = jax.nn.silu(cond).astype(jnp.bfloat16)
        moduls = [(matmul(silu_low[None, :], ada_flat[section_index])[0] + ada_b[section_index].reshape(6 * D)).reshape(6, D) for section_index in range(2)]
        first_out, first_saved = block_forward(tokens_in.astype(jnp.float32), moduls[0], params[0])
        first_low = rounded(first_out)
        second_out, second_saved = block_forward(first_low.astype(jnp.float32), moduls[1], params[1])
        second_low = second_out.astype(jnp.bfloat16)
        grad_second, grads_second, dmod_second = block_backward(cotangent.astype(jnp.float32), moduls[1], params[1], second_saved)
        grad_first, grads_first, dmod_first = block_backward(grad_second, moduls[0], params[0], first_saved)
        dmods = [dmod_first, dmod_second]
        new_grads = [grads_first, grads_second]
        cond_pull = jnp.zeros((D,), jnp.float32)
        new_ada = []
        new_adab = []
        for section_index in range(2):
            dmod_low = dmods[section_index].astype(jnp.bfloat16).reshape(1, 6 * D)
            new_ada.append(ada_grads[section_index] + matmul(silu_low[:, None], dmod_low))
            new_adab.append(adab_grads[section_index] + dmods[section_index])
            cond_pull = cond_pull + matmul(dmod_low, ada_flat[section_index].T)[0]
        cond_grad = jax.vjp(jax.nn.silu, cond)[1](cond_pull)[0]
        label_grad = label_grad.at[label_id].add(cond_grad)
        time_grad = time_grad.at[step_id].add(cond_grad)
        block_grads = tuple((tuple((left_arr + right_arr for left_arr, right_arr in zip(block_grads[section_index], new_grads[section_index]))) for section_index in range(2)))
        new_carry = (block_grads, tuple(new_ada), tuple(new_adab), label_grad, time_grad)
        return (new_carry, (first_low, second_low, grad_first, grad_second, cond_grad))
    items = (latents_in.reshape(LATENTS, SEQ, D), out_grad.reshape(LATENTS, SEQ, D), labels, timesteps)
    final, outputs = lax.scan(per_latent, carry_init, items)
    block_grads, ada_grads, adab_grads, label_grad, time_grad = final
    first_lows, second_lows, grad_firsts, grad_seconds, cond_grads = outputs
    block_outs = jnp.stack([first_lows.reshape(TOKENS, D), second_lows.reshape(TOKENS, D)])
    input_grads = jnp.stack([grad_firsts.reshape(TOKENS, D), grad_seconds.reshape(TOKENS, D)])
    ada_w_grad = jnp.stack([ada_grads[0].reshape(D, 6, D), ada_grads[1].reshape(D, 6, D)])
    ada_b_grad = jnp.stack([adab_grads[0], adab_grads[1]])
    stacked = [jnp.stack([block_grads[0][index_leaf], block_grads[1][index_leaf]]) for index_leaf in range(8)]
    return (block_outs, input_grads, cond_grads, label_grad, time_grad, ada_w_grad, ada_b_grad, stacked[0], stacked[1], stacked[2], stacked[3], stacked[4], stacked[5], stacked[6], stacked[7])
```

```python
import functools
import math

import jax
import jax.numpy as jnp
from jax import lax
from jax.experimental import pallas as pl
from jax.experimental.pallas import tpu as pltpu
from jax.sharding import PartitionSpec as P

D = 384
HALF = D // 2
HEADS = 6
HD = 64
FF = 1536
FFH = FF // 2
SEQ = 256
EPS = 1e-06
SCALE = 1.0 / math.sqrt(HD)
ROWS = 1152
GROWS = 1168
F32 = jnp.float32
BF16 = jnp.bfloat16


def dot(a, b):
    return jnp.dot(a, b, preferred_element_type=F32)


def dot_nt(a, b):
    return lax.dot_general(a, b, (((1,), (1,)), ((), ())), preferred_element_type=F32)


def dot_tn(a, b):
    return lax.dot_general(a, b, (((0,), (0,)), ((), ())), preferred_element_type=F32)


def shard_pieces(r, c):
    out = []
    for p, (pr, pc) in enumerate(((0, 0), (0, HALF), (HALF, 0))):
        out.append(("qkv", (c * HALF, HALF), (p * D + r * HALF, HALF), (pr, HALF), (pc, HALF)))
    out.append(("proj", (r * HALF, HALF), (c * HALF, HALF), (HALF, HALF), (HALF, HALF)))
    for k in range(2):
        out.append(("up", (c * HALF, HALF), (r * FFH + k * D, D), (D + k * HALF, HALF), (0, D)))
        out.append(("down", (r * FFH + k * D, D), (c * HALF, HALF), (2 * D, D), (k * HALF, HALF)))
    return out


def span(pair):
    return slice(pair[0], pair[0] + pair[1])


def norm_rows(v):
    mean_val = jnp.mean(v, axis=-1, keepdims=True)
    cen = v - mean_val
    inv = lax.rsqrt(jnp.mean(cen * cen, axis=-1, keepdims=True) + EPS)
    return cen * inv, inv


def norm_back(g, normed, inv):
    return inv * (
        g
        - jnp.mean(g, axis=-1, keepdims=True)
        - normed * jnp.mean(g * normed, axis=-1, keepdims=True)
    )


C0 = math.sqrt(2.0 / math.pi)


def gelu_parts(v):
    t = jnp.tanh(C0 * (v + 0.044715 * (v * v * v)))
    return 0.5 * v * (1.0 + t), t


def gelu_slope(v, t):
    return 0.5 * (1.0 + t) + 0.5 * v * (1.0 - t * t) * (C0 * (1.0 + 3.0 * 0.044715 * (v * v)))


def softmax(q, k):
    s = dot_nt(q, k) * SCALE
    e = jnp.exp(s - jnp.max(s, axis=-1, keepdims=True))
    return e * (1.0 / jnp.sum(e, axis=-1, keepdims=True))


def head(arr, part, h):
    at = part * D + h * HD
    return arr[:, at : at + HD]


def forward(x, mod, w, b, keep=None):
    def put(name, value):
        if keep is not None:
            keep[name][...] = value

    m = [mod[i : i + 1, :] for i in range(6)]
    normed1, inv1 = norm_rows(x)
    hidden1 = (normed1 * (1.0 + m[1]) + m[0]).astype(BF16)
    packed = (dot(hidden1, w["qkv"][...]) + b["qkv"]).astype(BF16)
    heads = []
    for h in range(HEADS):
        prob = softmax(head(packed, 0, h), head(packed, 1, h))
        heads.append(dot(prob.astype(BF16), head(packed, 2, h)).astype(BF16))
        if keep is not None:
            keep["prob"][h] = prob
    attended = jnp.concatenate(heads, axis=1)
    branch_a = dot(attended, w["proj"][...]) + b["proj"]
    middle = x + m[2] * branch_a
    normed2, inv2 = norm_rows(middle)
    hidden2 = (normed2 * (1.0 + m[4]) + m[3]).astype(BF16)
    pre = dot(hidden2, w["up"][...]) + b["up"]
    act, _ = gelu_parts(pre)
    act = act.astype(BF16)
    branch_f = dot(act, w["down"][...]) + b["down"]
    put("normed1", normed1)
    put("inv1", inv1)
    put("hidden1", hidden1)
    put("packed", packed)
    put("attended", attended)
    put("branch_a", branch_a)
    put("normed2", normed2)
    put("inv2", inv2)
    put("hidden2", hidden2)
    put("pre", pre)
    put("act", act)
    put("branch_f", branch_f)
    return (middle + m[5] * branch_f).astype(BF16)


SAVES = (
    ("normed1", (SEQ, D), F32),
    ("inv1", (SEQ, 1), F32),
    ("hidden1", (SEQ, D), BF16),
    ("packed", (SEQ, 3 * D), BF16),
    ("prob", (HEADS, SEQ, SEQ), F32),
    ("attended", (SEQ, D), BF16),
    ("branch_a", (SEQ, D), F32),
    ("normed2", (SEQ, D), F32),
    ("inv2", (SEQ, 1), F32),
    ("hidden2", (SEQ, D), BF16),
    ("pre", (SEQ, FF), F32),
    ("act", (SEQ, FF), BF16),
    ("branch_f", (SEQ, D), F32),
)
WEIGHTS = (("qkv", (D, 3 * D)), ("proj", (D, D)), ("up", (D, FF)), ("down", (FF, D)))


def col_sum(v):
    return jnp.sum(v.astype(F32), axis=0, keepdims=True)


def backward(grad_out, mod, w, s, put_w=None, put_b=None, dmod=None):
    full = put_w is not None
    m = [mod[i : i + 1, :] for i in range(6)]
    grad_f = (grad_out * m[5]).astype(BF16)
    pre = s["pre"][...]
    _, t = gelu_parts(pre)
    grad_pre = (dot_nt(grad_f, w["down"][...]) * gelu_slope(pre, t)).astype(BF16)
    if full:
        dmod[5:6, :] = col_sum(grad_out * s["branch_f"][...])
        put_w("down", dot_tn(s["act"][...], grad_f).astype(BF16))
        put_b("down", col_sum(grad_f))
    grad_h2 = dot_nt(grad_pre, w["up"][...])
    normed2 = s["normed2"][...]
    if full:
        put_w("up", dot_tn(s["hidden2"][...], grad_pre).astype(BF16))
        put_b("up", col_sum(grad_pre))
        dmod[4:5, :] = col_sum(grad_h2 * normed2)
        dmod[3:4, :] = col_sum(grad_h2)
    grad_mid = grad_out + norm_back(grad_h2 * (1.0 + m[4]), normed2, s["inv2"][...])
    grad_a = (grad_mid * m[2]).astype(BF16)
    if full:
        dmod[2:3, :] = col_sum(grad_mid * s["branch_a"][...])
        put_w("proj", dot_tn(s["attended"][...], grad_a).astype(BF16))
        put_b("proj", col_sum(grad_a))
    grad_att = dot_nt(grad_a, w["proj"][...]).astype(BF16)
    packed = s["packed"][...]
    parts = [[], [], []]
    for h in range(HEADS):
        q, k, v = (head(packed, i, h) for i in range(3))
        prob = s["prob"][h]
        g = grad_att[:, h * HD : (h + 1) * HD]
        grad_prob = dot_nt(g, v)
        delta = jnp.sum(prob * grad_prob, axis=-1, keepdims=True)
        gs = (prob * (grad_prob - delta) * SCALE).astype(BF16)
        parts[0].append(dot(gs, k).astype(BF16))
        parts[1].append(dot_tn(gs, q).astype(BF16))
        parts[2].append(dot_tn(prob.astype(BF16), g).astype(BF16))
    grad_packed = jnp.concatenate(parts[0] + parts[1] + parts[2], axis=1)
    normed1 = s["normed1"][...]
    grad_h1 = dot_nt(grad_packed, w["qkv"][...])
    if full:
        put_w("qkv", dot_tn(s["hidden1"][...], grad_packed).astype(BF16))
        put_b("qkv", col_sum(grad_packed))
        dmod[1:2, :] = col_sum(grad_h1 * normed1)
        dmod[0:1, :] = col_sum(grad_h1)
    return grad_mid + norm_back(grad_h1 * (1.0 + m[1]), normed1, s["inv1"][...])


def first_kernel(x_ref, mod_ref, bq, bp, bu, bd, shards, out_ref, wq, wp, wu, wd):
    w = dict(qkv=wq, proj=wp, up=wu, down=wd)
    for r in range(2):
        for c in range(2):
            for name, fr, fc, pr, pc in shard_pieces(r, c):
                w[name][span(fr), span(fc)] = shards[2 * r + c, span(pr), span(pc)]
    b = dict(qkv=bq[...], proj=bp[...], up=bu[...], down=bd[...])
    out_ref[...] = forward(x_ref[...].astype(F32), mod_ref, w, b)


def second_kernel(x_ref, g_ref, mod_ref, bq, bp, bu, bd, wq, wp, wu, wd, out_ref, gin_ref, *saves):
    w = dict(qkv=wq, proj=wp, up=wu, down=wd)
    s = {name: ref for (name, _, _), ref in zip(SAVES, saves)}
    b = dict(qkv=bq[...], proj=bp[...], up=bu[...], down=bd[...])
    out_ref[...] = forward(x_ref[...].astype(F32), mod_ref, w, b, s)
    gin_ref[...] = backward(g_ref[...].astype(F32), mod_ref, w, s).astype(BF16)


def third_kernel(g_ref, mod_ref, wq, wp, wu, wd, *rest):
    w = dict(qkv=wq, proj=wp, up=wu, down=wd)
    n = len(SAVES)
    s = {name: ref for (name, _, _), ref in zip(SAVES, rest[:n])}
    gin_ref, packed_ref, dmod_ref = rest[n:]
    packed_ref[:, ROWS:, :] = jnp.zeros((4, GROWS - ROWS, D), BF16)

    def put_w(name, value):
        for r in range(2):
            for c in range(2):
                for piece, fr, fc, pr, pc in shard_pieces(r, c):
                    if piece == name:
                        packed_ref[2 * r + c, span(pr), span(pc)] = value[span(fr), span(fc)]

    biases = {}
    put_b = biases.__setitem__
    gin_ref[...] = backward(g_ref[...].astype(F32), mod_ref, w, s, put_w, put_b, dmod_ref)
    zero = jnp.zeros((1, HALF), F32)
    for r in range(2):
        for c in range(2):
            bq = [biases["qkv"][:, p * D + r * HALF : p * D + (r + 1) * HALF] for p in range(3)]
            rows = [
                jnp.concatenate(bq[:2], axis=1),
                jnp.concatenate([bq[2], biases["proj"][:, c * HALF : (c + 1) * HALF]], axis=1),
                biases["up"][:, r * FFH : r * FFH + D],
                biases["up"][:, r * FFH + D : (r + 1) * FFH],
                jnp.concatenate([biases["down"][:, c * HALF : (c + 1) * HALF], zero], axis=1),
                jnp.zeros((GROWS - ROWS - 5, D), F32),
            ]
            packed_ref[2 * r + c, ROWS:, :] = jnp.concatenate(rows, axis=0).astype(BF16)


def call(body, outs, args, flops=2_000_000_000):
    vmem = pl.BlockSpec(memory_space=pltpu.VMEM)
    return pl.pallas_call(
        body,
        out_shape=[jax.ShapeDtypeStruct(s, d) for s, d in outs],
        in_specs=[vmem] * len(args),
        out_specs=[vmem] * len(outs),
        compiler_params=pltpu.CompilerParams(vmem_limit_bytes=60 * 1024 * 1024),
        cost_estimate=pl.CostEstimate(flops=flops, bytes_accessed=8_000_000, transcendentals=800_000),
    )(*args)


def pack(qkv, proj, up, down):
    qkv = qkv.reshape(HALF, 3 * HALF)
    return jnp.concatenate(
        [
            qkv[:, :D],
            jnp.concatenate([qkv[:, D:], proj], axis=1),
            up[:, :D],
            up[:, D:],
            jnp.concatenate([down[:D], down[D:]], axis=1),
        ],
        axis=0,
    )


def on_device(
    latents_in,
    labels,
    timesteps,
    out_grad,
    label_table,
    time_table,
    ada_w,
    ada_b,
    qkv_w,
    qkv_b,
    proj_w,
    proj_b,
    fc1_w,
    fc1_b,
    fc2_w,
    fc2_b,
):
    section_zero = lax.axis_index("section") == 0
    col = lax.axis_index("col")
    swap = [(0, 1), (1, 0)]

    def exchange(a):
        n = a.shape[0] // 2
        mine = lax.dynamic_slice_in_dim(a, col * n, n, 0)
        theirs = lax.ppermute(lax.dynamic_slice_in_dim(a, (1 - col) * n, n, 0), "col", swap)
        first = jnp.where(col == 0, mine, theirs)
        second = jnp.where(col == 0, theirs, mine)
        return jnp.concatenate([first, second], axis=-1)

    def unexchange(a):
        half = a.shape[-1] // 2
        mine = lax.dynamic_slice_in_dim(a, col * half, half, 1)
        theirs = lax.ppermute(lax.dynamic_slice_in_dim(a, (1 - col) * half, half, 1), "col", swap)
        first = jnp.where(col == 0, mine, theirs)
        second = jnp.where(col == 0, theirs, mine)
        return jnp.concatenate([first, second], axis=0)

    shards = lax.all_gather(pack(qkv_w[0], proj_w[0], fc1_w[0], fc2_w[0]), ("row", "col"), axis=0)
    own = latents_in.shape[0] // SEQ
    cond = jnp.concatenate(
        [
            lax.dynamic_slice_in_dim(label_table, labels[i], 1, 0).astype(F32)
            + lax.dynamic_slice_in_dim(time_table, timesteps[i], 1, 0).astype(F32)
            for i in range(own)
        ],
        axis=0,
    )
    silu_low = jax.nn.silu(cond).astype(BF16)
    ada_flat = ada_w[0].reshape(D, 6 * HALF)
    modul_half = dot(silu_low, ada_flat) + ada_b[0].reshape(6 * HALF)
    small = jnp.concatenate(
        [
            modul_half.reshape(own * 6 * HALF),
            qkv_b[0].reshape(3 * HALF),
            proj_b[0],
            fc1_b[0],
            fc2_b[0],
        ]
    )
    everyone = lax.all_gather(small, ("row", "col"), axis=0).reshape(2, 2, -1)
    row = lax.axis_index("row")
    own_row = lax.dynamic_index_in_dim(everyone, row, 0, keepdims=False)
    mods = own_row[:, : own * 6 * HALF].reshape(2, own, 6, HALF)
    mods = lax.dynamic_index_in_dim(mods, col, 1, keepdims=False)
    mod = jnp.concatenate([mods[0], mods[1]], axis=-1)
    at = own * 6 * HALF
    b_qkv = jnp.transpose(everyone[:, 0, at : at + 3 * HALF].reshape(2, 3, HALF), (1, 0, 2)).reshape(1, 3 * D)
    at += 3 * HALF
    b_proj = everyone[0, :, at : at + HALF].reshape(1, D)
    at += HALF
    b_up = everyone[:, 0, at : at + FFH].reshape(1, FF)
    at += FFH
    b_down = everyone[0, :, at : at + HALF].reshape(1, D)
    b = (b_qkv, b_proj, b_up, b_down)

    x = exchange(latents_in)
    cot = exchange(out_grad)
    out1, *w = call(
        first_kernel,
        [((SEQ, D), BF16)] + [(s, BF16) for _, s in WEIGHTS],
        (x, mod, *b, shards),
    )
    received = lax.ppermute(out1, "section", [(0, 1)])
    x2 = jnp.where(section_zero, x, received)
    out, gin1, *saves = call(
        second_kernel,
        [((SEQ, D), BF16), ((SEQ, D), BF16)] + [(s, d) for _, s, d in SAVES],
        (x2, cot, mod, *b, *w),
    )
    grad_back = lax.ppermute(gin1, "section", [(1, 0)])
    cot2 = jnp.where(section_zero, grad_back, cot)
    gin, packed, dmod = call(
        third_kernel,
        [((SEQ, D), F32), ((4, GROWS, D), BF16), ((6, D), F32)],
        (cot2, mod, *w, *saves),
    )
    reduced = lax.psum_scatter(packed, ("row", "col"), scatter_dimension=0, tiled=True)
    reduced = lax.psum(reduced, "dp")[0].astype(F32)

    block_outs = unexchange(out)
    input_grads = unexchange(gin)
    dmod_flat = unexchange(dmod).reshape(own, 6 * HALF)
    dmod_low = dmod_flat.astype(BF16)
    cond_pull = lax.psum(dot_nt(dmod_low, ada_flat), ("section", "col"))
    cond_grad = jax.vjp(jax.nn.silu, cond)[1](cond_pull)[0]
    ids = jnp.stack([labels, timesteps], axis=1)
    ids_all = lax.all_gather(ids, ("dp", "row"), axis=0, tiled=True)
    piece = lax.all_gather(
        jnp.concatenate([cond_grad, dmod_flat, silu_low.astype(F32)], axis=1), ("dp", "row"), axis=0, tiled=True
    )
    grad_piece = piece[:, :D]
    dmod_piece = piece[:, D : D + 6 * HALF]
    silu_piece = piece[:, D + 6 * HALF :].astype(BF16)
    ada_sum = dot_tn(silu_piece, dmod_piece.astype(BF16))
    adab_sum = jnp.sum(dmod_piece, axis=0)

    def table_sum(ids, count):
        hot = (ids[:, None] == jnp.arange(count, dtype=jnp.int32)[None, :]).astype(F32)
        return jnp.einsum("nc,na->ca", hot, grad_piece, precision=lax.Precision.HIGHEST)

    g_qkv = jnp.concatenate([reduced[:HALF], reduced[HALF:D, :HALF]], axis=1)
    g_proj = reduced[HALF:D, HALF:]
    g_up = jnp.concatenate([reduced[D : D + HALF], reduced[D + HALF : 2 * D]], axis=1)
    g_down = jnp.concatenate([reduced[2 * D : 3 * D, :HALF], reduced[2 * D : 3 * D, HALF:]], axis=0)
    tail = reduced[ROWS:]
    return (
        block_outs[None],
        input_grads[None],
        cond_grad,
        table_sum(ids_all[:, 0], label_table.shape[0]),
        table_sum(ids_all[:, 1], time_table.shape[0]),
        ada_sum.reshape(D, 6, HALF)[None],
        adab_sum.reshape(6, HALF)[None],
        g_qkv.reshape(HALF, 3, HALF)[None],
        jnp.concatenate([tail[0], tail[1, :HALF]]).reshape(3, HALF)[None],
        g_proj[None],
        tail[1, HALF:][None],
        g_up[None],
        jnp.concatenate([tail[2], tail[3]])[None],
        g_down[None],
        tail[4, :HALF][None],
    )


def solution(mesh):
    return jax.shard_map(
        on_device,
        mesh=mesh,
        in_specs=(
            P(("dp", "row"), "col"),
            P(("dp", "row")),
            P(("dp", "row")),
            P(("dp", "row"), "col"),
            P(),
            P(),
            P("section", None, None, "col"),
            P("section", None, "col"),
            P("section", "col", None, "row"),
            P("section", None, "row"),
            P("section", "row", "col"),
            P("section", "col"),
            P("section", "col", "row"),
            P("section", "row"),
            P("section", "row", "col"),
            P("section", "col"),
        ),
        out_specs=(
            P("section", ("dp", "row"), "col"),
            P("section", ("dp", "row"), "col"),
            P(("dp", "row"), None),
            P(),
            P(),
            P("section", None, None, "col"),
            P("section", None, "col"),
            P("section", "col", None, "row"),
            P("section", None, "row"),
            P("section", "row", "col"),
            P("section", "col"),
            P("section", "col", "row"),
            P("section", "row"),
            P("section", "row", "col"),
            P("section", "col"),
        ),
        check_vma=False,
    )
```

```python
import functools
import math

import jax
import jax.numpy as jnp
from jax import lax
from jax.experimental import pallas as pl
from jax.experimental.pallas import tpu as pltpu
from jax.sharding import PartitionSpec as P

D = 384
HALF = D // 2
HEADS = 6
HD = 64
FF = 1536
FFH = FF // 2
SEQ = 256
EPS = 1e-06
SCALE = 1.0 / math.sqrt(HD)
ROWS = 1152
GROWS = 1184
CHUNKS = ((0, 320), (320, 320), (640, 288), (928, 256))
MESH = pl.DeviceIdType.MESH
F32 = jnp.float32
BF16 = jnp.bfloat16


def dot(a, b):
    return jnp.dot(a, b, preferred_element_type=F32)


def dot_nt(a, b):
    return lax.dot_general(a, b, (((1,), (1,)), ((), ())), preferred_element_type=F32)


def dot_tn(a, b):
    return lax.dot_general(a, b, (((0,), (0,)), ((), ())), preferred_element_type=F32)


def shard_pieces(r, c):
    out = []
    for p, (pr, pc) in enumerate(((0, 0), (0, HALF), (HALF, 0))):
        out.append(("qkv", (c * HALF, HALF), (p * D + r * HALF, HALF), (pr, HALF), (pc, HALF)))
    out.append(("proj", (r * HALF, HALF), (c * HALF, HALF), (HALF, HALF), (HALF, HALF)))
    for k in range(2):
        out.append(("up", (c * HALF, HALF), (r * FFH + k * D, D), (D + k * HALF, HALF), (0, D)))
        out.append(("down", (r * FFH + k * D, D), (c * HALF, HALF), (2 * D, D), (k * HALF, HALF)))
    return out


def span(pair):
    return slice(pair[0], pair[0] + pair[1])


def norm_rows(v):
    mean_val = jnp.mean(v, axis=-1, keepdims=True)
    cen = v - mean_val
    inv = lax.rsqrt(jnp.mean(cen * cen, axis=-1, keepdims=True) + EPS)
    return cen * inv, inv


def norm_back(g, normed, inv):
    return inv * (
        g
        - jnp.mean(g, axis=-1, keepdims=True)
        - normed * jnp.mean(g * normed, axis=-1, keepdims=True)
    )


C0 = math.sqrt(2.0 / math.pi)


def gelu_parts(v):
    t = jnp.tanh(C0 * (v + 0.044715 * (v * v * v)))
    return 0.5 * v * (1.0 + t), t


def gelu_slope(v, t):
    return 0.5 * (1.0 + t) + 0.5 * v * (1.0 - t * t) * (C0 * (1.0 + 3.0 * 0.044715 * (v * v)))


def softmax(q, k):
    s = dot_nt(q, k) * SCALE
    e = jnp.exp(s - jnp.max(s, axis=-1, keepdims=True))
    return e * (1.0 / jnp.sum(e, axis=-1, keepdims=True))


def head(arr, part, h):
    at = part * D + h * HD
    return arr[:, at : at + HD]


def forward(x, mod, w, b, keep=None):
    def put(name, value):
        if keep is not None:
            keep[name][...] = value

    m = [mod[i : i + 1, :] for i in range(6)]
    normed1, inv1 = norm_rows(x)
    hidden1 = (normed1 * (1.0 + m[1]) + m[0]).astype(BF16)
    packed = (dot(hidden1, w["qkv"][...]) + b["qkv"]).astype(BF16)
    heads = []
    for h in range(HEADS):
        prob = softmax(head(packed, 0, h), head(packed, 1, h))
        heads.append(dot(prob.astype(BF16), head(packed, 2, h)).astype(BF16))
        if keep is not None:
            keep["prob"][h] = prob
    attended = jnp.concatenate(heads, axis=1)
    branch_a = dot(attended, w["proj"][...]) + b["proj"]
    middle = x + m[2] * branch_a
    normed2, inv2 = norm_rows(middle)
    hidden2 = (normed2 * (1.0 + m[4]) + m[3]).astype(BF16)
    pre = dot(hidden2, w["up"][...]) + b["up"]
    act, _ = gelu_parts(pre)
    act = act.astype(BF16)
    branch_f = dot(act, w["down"][...]) + b["down"]
    put("normed1", normed1)
    put("inv1", inv1)
    put("hidden1", hidden1)
    put("packed", packed)
    put("attended", attended)
    put("branch_a", branch_a)
    put("normed2", normed2)
    put("inv2", inv2)
    put("hidden2", hidden2)
    put("pre", pre)
    put("act", act)
    put("branch_f", branch_f)
    return (middle + m[5] * branch_f).astype(BF16)


SAVES = (
    ("normed1", (SEQ, D), F32),
    ("inv1", (SEQ, 1), F32),
    ("hidden1", (SEQ, D), BF16),
    ("packed", (SEQ, 3 * D), BF16),
    ("prob", (HEADS, SEQ, SEQ), F32),
    ("attended", (SEQ, D), BF16),
    ("branch_a", (SEQ, D), F32),
    ("normed2", (SEQ, D), F32),
    ("inv2", (SEQ, 1), F32),
    ("hidden2", (SEQ, D), BF16),
    ("pre", (SEQ, FF), F32),
    ("act", (SEQ, FF), BF16),
    ("branch_f", (SEQ, D), F32),
)
WEIGHTS = (("qkv", (D, 3 * D)), ("proj", (D, D)), ("up", (D, FF)), ("down", (FF, D)))


def col_sum(v):
    return jnp.sum(v.astype(F32), axis=0, keepdims=True)


def backward(grad_out, mod, w, s, put_w=None, put_b=None, dmod=None):
    full = put_w is not None
    m = [mod[i : i + 1, :] for i in range(6)]
    grad_f = (grad_out * m[5]).astype(BF16)
    pre = s["pre"][...]
    _, t = gelu_parts(pre)
    grad_pre = (dot_nt(grad_f, w["down"][...]) * gelu_slope(pre, t)).astype(BF16)
    if full:
        dmod[5] = col_sum(grad_out * s["branch_f"][...])
        put_w("down", dot_tn(s["act"][...], grad_f).astype(BF16))
        put_b("down", col_sum(grad_f))
    grad_h2 = dot_nt(grad_pre, w["up"][...])
    normed2 = s["normed2"][...]
    if full:
        put_w("up", dot_tn(s["hidden2"][...], grad_pre).astype(BF16))
        put_b("up", col_sum(grad_pre))
        dmod[4] = col_sum(grad_h2 * normed2)
        dmod[3] = col_sum(grad_h2)
    grad_mid = grad_out + norm_back(grad_h2 * (1.0 + m[4]), normed2, s["inv2"][...])
    grad_a = (grad_mid * m[2]).astype(BF16)
    if full:
        dmod[2] = col_sum(grad_mid * s["branch_a"][...])
        put_w("proj", dot_tn(s["attended"][...], grad_a).astype(BF16))
        put_b("proj", col_sum(grad_a))
    grad_att = dot_nt(grad_a, w["proj"][...]).astype(BF16)
    packed = s["packed"][...]
    parts = [[], [], []]
    for h in range(HEADS):
        q, k, v = (head(packed, i, h) for i in range(3))
        prob = s["prob"][h]
        g = grad_att[:, h * HD : (h + 1) * HD]
        grad_prob = dot_nt(g, v)
        delta = jnp.sum(prob * grad_prob, axis=-1, keepdims=True)
        gs = (prob * (grad_prob - delta) * SCALE).astype(BF16)
        parts[0].append(dot(gs, k).astype(BF16))
        parts[1].append(dot_tn(gs, q).astype(BF16))
        parts[2].append(dot_tn(prob.astype(BF16), g).astype(BF16))
    grad_packed = jnp.concatenate(parts[0] + parts[1] + parts[2], axis=1)
    normed1 = s["normed1"][...]
    grad_h1 = dot_nt(grad_packed, w["qkv"][...])
    if full:
        put_w("qkv", dot_tn(s["hidden1"][...], grad_packed).astype(BF16))
        put_b("qkv", col_sum(grad_packed))
        dmod[1] = col_sum(grad_h1 * normed1)
        dmod[0] = col_sum(grad_h1)
    return grad_mid + norm_back(grad_h1 * (1.0 + m[1]), normed1, s["inv1"][...])


def first_kernel(x_ref, mod_ref, bq, bp, bu, bd, shards, out_ref, wq, wp, wu, wd):
    w = dict(qkv=wq, proj=wp, up=wu, down=wd)
    for r in range(2):
        for c in range(2):
            for name, fr, fc, pr, pc in shard_pieces(r, c):
                w[name][span(fr), span(fc)] = shards[2 * r + c, span(pr), span(pc)]
    b = dict(qkv=bq[...], proj=bp[...], up=bu[...], down=bd[...])
    out_ref[...] = forward(x_ref[...].astype(F32), mod_ref, w, b)


def second_kernel(x_ref, g_ref, mod_ref, bq, bp, bu, bd, wq, wp, wu, wd, out_ref, gin_ref, *saves):
    w = dict(qkv=wq, proj=wp, up=wu, down=wd)
    s = {name: ref for (name, _, _), ref in zip(SAVES, saves)}
    b = dict(qkv=bq[...], proj=bp[...], up=bu[...], down=bd[...])
    out = forward(x_ref[...].astype(F32), mod_ref, w, b, s)
    for c in range(2):
        out_ref[c] = out[:, c * HALF : (c + 1) * HALF]
    gin_ref[...] = backward(g_ref[...].astype(F32), mod_ref, w, s).astype(BF16)


def third_kernel(g_ref, mod_ref, wq, wp, wu, wd, *rest):
    w = dict(qkv=wq, proj=wp, up=wu, down=wd)
    n = len(SAVES)
    s = {name: ref for (name, _, _), ref in zip(SAVES, rest[:n])}
    gin_ref, packed_ref, dmod_ref = rest[n:]
    packed_ref[:, ROWS:, :] = jnp.zeros((4, GROWS - ROWS, D), BF16)

    def put_w(name, value):
        for r in range(2):
            for c in range(2):
                for piece, fr, fc, pr, pc in shard_pieces(r, c):
                    if piece == name:
                        packed_ref[2 * r + c, span(pr), span(pc)] = value[span(fr), span(fc)]

    biases = {}
    put_b = biases.__setitem__
    dmod_ref[...] = jnp.zeros_like(dmod_ref)
    dmod = {}
    gin = backward(g_ref[...].astype(F32), mod_ref, w, s, put_w, put_b, dmod)
    for c in range(2):
        gin_ref[c] = gin[:, c * HALF : (c + 1) * HALF]
        for i in range(6):
            dmod_ref[c, i : i + 1, :] = dmod[i][:, c * HALF : (c + 1) * HALF]
    zero = jnp.zeros((1, HALF), F32)
    for r in range(2):
        for c in range(2):
            bq = [biases["qkv"][:, p * D + r * HALF : p * D + (r + 1) * HALF] for p in range(3)]
            rows = [
                jnp.concatenate(bq[:2], axis=1),
                jnp.concatenate([bq[2], biases["proj"][:, c * HALF : (c + 1) * HALF]], axis=1),
                biases["up"][:, r * FFH : r * FFH + D],
                biases["up"][:, r * FFH + D : (r + 1) * FFH],
                jnp.concatenate([biases["down"][:, c * HALF : (c + 1) * HALF], zero], axis=1),
                jnp.zeros((GROWS - ROWS - 5, D), F32),
            ]
            packed_ref[2 * r + c, ROWS:, :] = jnp.concatenate(rows, axis=0).astype(BF16)


def call(body, outs, args, flops=2_000_000_000):
    vmem = pl.BlockSpec(memory_space=pltpu.VMEM)
    return pl.pallas_call(
        body,
        out_shape=[jax.ShapeDtypeStruct(s, d) for s, d in outs],
        in_specs=[vmem] * len(args),
        out_specs=[vmem] * len(outs),
        compiler_params=pltpu.CompilerParams(vmem_limit_bytes=60 * 1024 * 1024),
        cost_estimate=pl.CostEstimate(flops=flops, bytes_accessed=8_000_000, transcendentals=800_000),
    )(*args)


def flipped(index, step):
    return index + step * (1 - 2 * lax.rem(index // step, 2))


def greet(partners):
    barrier = pltpu.get_barrier_semaphore()
    for where in partners:
        pl.semaphore_signal(barrier, inc=1, device_id=where, device_id_type=MESH)
    pl.semaphore_wait(barrier, len(partners))


class Wires:
    def __init__(self, send_sem, recv_sem):
        self.send_sem, self.recv_sem, self.started = send_sem, recv_sem, []

    def send(self, k, src, dst, where):
        copy = pltpu.make_async_remote_copy(
            src_ref=src,
            dst_ref=dst,
            send_sem=self.send_sem.at[k],
            recv_sem=self.recv_sem.at[k],
            device_id=where,
            device_id_type=MESH,
        )
        copy.start()
        self.started.append(copy)

    def arrived(self, k, dst, where):
        pltpu.make_async_remote_copy(
            src_ref=dst,
            dst_ref=dst,
            send_sem=self.send_sem.at[k],
            recv_sem=self.recv_sem.at[k],
            device_id=where,
            device_id_type=MESH,
        ).wait_recv()

    def finish(self):
        for copy in self.started:
            copy.wait_send()


PIECE = 192
PIECES = ROWS // 2 // PIECE


def gather_kernel(
    shard, lat, cot, labels, times, ltab, ttab, ada, adab, bias,
    out, x_out, cot_out, mod_out, bias_out, silu_out, cond_out,
    xr, cr, modbuf, biasbuf, send_sem, recv_sem,
):
    r, c, z = lax.axis_index("row"), lax.axis_index("col"), lax.axis_index("dp")
    h = lax.rem(z, 2)
    to_col, to_row, to_dp = {"col": 1 - c}, {"row": 1 - r}, {"dp": flipped(z, 1)}
    greet((to_col, to_row, to_dp))
    wires = Wires(send_sem, recv_sem)
    own, facing = 2 * r + c, 2 * (1 - r) + c

    def rows(half, i):
        return pl.ds(pl.multiple_of(half * (ROWS // 2) + i * PIECE, PIECE), PIECE)

    for i in range(PIECES):
        wires.send(i, shard.at[rows(h, i)], out.at[own, rows(h, i)], to_row)
    theirs = pl.ds(pl.multiple_of((1 - c) * SEQ, SEQ), SEQ)
    mine = pl.ds(pl.multiple_of(c * SEQ, SEQ), SEQ)
    base = 2 * PIECES
    wires.send(base, lat.at[theirs], xr.at[c], to_col)
    wires.send(base + 1, cot.at[theirs], cr.at[c], to_col)
    wires.send(base + 2, shard, out.at[own], to_col)
    wires.send(base + 3, bias, biasbuf.at[0], to_col)
    wires.send(base + 4, bias, biasbuf.at[1], to_row)
    out[own] = shard[...]
    xr[c] = lat[mine, :]
    cr[c] = cot[mine, :]

    def hot(ids, table):
        grid = lax.broadcasted_iota(jnp.int32, (ids.shape[0], table.shape[0]), 1)
        return dot(jnp.where(grid == ids[...], 1.0, 0.0).astype(BF16), table[...])

    cond = hot(labels, ltab) + hot(times, ttab)
    cond_out[...] = cond
    silu_low = (cond / (1.0 + jnp.exp(-cond))).astype(BF16)
    silu_out[...] = silu_low.astype(F32)
    modul = dot(silu_low, ada[...]) + adab[...]
    modbuf[0:2] = jnp.zeros((2, 8, HALF), F32)
    for latent in range(2):
        for i in range(6):
            modbuf[latent, i : i + 1, :] = modul[latent : latent + 1, i * HALF : (i + 1) * HALF]
    far = base + 6
    for i in range(PIECES):
        wires.arrived(i, out.at[facing, rows(h, i)], to_row)
        wires.send(PIECES + i, out.at[facing, rows(h, i)], out.at[facing, rows(h, i)], to_dp)
        wires.send(far + i, out.at[facing, rows(h, i)], out.at[facing, rows(h, i)], to_col)
        if i == 0:
            wires.send(base + 5, modbuf.at[1 - c], modbuf.at[2 + c], to_col)
    for i in range(PIECES):
        wires.arrived(PIECES + i, out.at[facing, rows(1 - h, i)], to_dp)
        wires.send(far + PIECES + i, out.at[facing, rows(1 - h, i)], out.at[facing, rows(1 - h, i)], to_col)
    wires.arrived(base, xr.at[1 - c], to_col)
    wires.arrived(base + 1, cr.at[1 - c], to_col)
    wires.arrived(base + 3, biasbuf.at[0], to_col)
    wires.arrived(base + 4, biasbuf.at[1], to_row)
    wires.arrived(base + 5, modbuf.at[2 + 1 - c], to_col)
    modbuf[2 + c] = modbuf[c]
    bias_out[...] = biasbuf[...]
    for half in range(2):
        x_out[:, half * HALF : (half + 1) * HALF] = xr[half]
        cot_out[:, half * HALF : (half + 1) * HALF] = cr[half]
        mod_out[:, half * HALF : (half + 1) * HALF] = modbuf[2 + half]
    wires.arrived(base + 2, out.at[2 * r + 1 - c], to_col)
    for i in range(PIECES):
        wires.arrived(far + i, out.at[2 * (1 - r) + 1 - c, rows(h, i)], to_col)
    for i in range(PIECES):
        wires.arrived(far + PIECES + i, out.at[2 * (1 - r) + 1 - c, rows(1 - h, i)], to_col)
    wires.finish()


def reduce_kernel(
    bits, packed, outs, gin, dmod, cond, silu, labels, times, ada,
    g_qkv, g_proj, g_up, g_down, tail, block_out, input_grad, table, cond_grad,
    rc, t1, own1, rr, t2, acc, rz, res, dm, pull, send_sem, recv_sem,
):
    r, c, z = lax.axis_index("row"), lax.axis_index("col"), lax.axis_index("dp")
    b = lax.rem(z, 2)
    sec = lax.axis_index("section")
    to_col, to_row, to_sec = {"col": 1 - c}, {"row": 1 - r}, {"section": 1 - sec}
    to_dp = [{"dp": flipped(z, 1 << j)} for j in range(bits)]
    greet((to_col, to_row, to_sec, *to_dp))
    wires = Wires(send_sem, recv_sem)
    count = len(CHUNKS)
    number = iter(range(1000))
    n_col = [[next(number) for _ in range(2)] for _ in CHUNKS]
    n_row = [next(number) for _ in CHUNKS]
    n_dp = [[next(number) for _ in range(bits)] for _ in CHUNKS]
    n_back = [next(number) for _ in CHUNKS]
    n_dm, n_p0, n_p1, n_out, n_gin = (next(number) for _ in range(5))
    n_table = [next(number) for _ in range(bits + 1)]

    def rows(k):
        return pl.ds(CHUNKS[k][0], CHUNKS[k][1])

    def half(k, which):
        size = CHUNKS[k][1] // 2
        return pl.ds(pl.multiple_of(CHUNKS[k][0] + which * size, 16), size)

    wires.send(n_dm, dmod.at[1 - c], dm.at[c], to_col)
    for k in range(count):
        for which, q in enumerate((1 - r, r)):
            wires.send(n_col[k][which], packed.at[2 * q + 1 - c, rows(k)], rc.at[q, rows(k)], to_col)
    mine = pl.ds(pl.multiple_of(c * SEQ, SEQ), SEQ)
    others = pl.ds(pl.multiple_of((1 - c) * SEQ, SEQ), SEQ)
    wires.send(n_out, outs.at[1 - c], block_out.at[mine], to_col)
    wires.send(n_gin, gin.at[1 - c], input_grad.at[mine], to_col)

    def total(left, right):
        return (left.astype(F32) + right.astype(F32)).astype(BF16)

    def from_col(k):
        wires.arrived(n_col[k][0], rc.at[1 - r, rows(k)], to_col)
        t1[rows(k), :] = total(packed[2 * (1 - r) + c, rows(k), :], rc[1 - r, rows(k), :])
        wires.send(n_row[k], t1.at[rows(k)], rr.at[rows(k)], to_row)
        wires.arrived(n_col[k][1], rc.at[r, rows(k)], to_col)
        own1[rows(k), :] = total(packed[2 * r + c, rows(k), :], rc[r, rows(k), :])

    def from_row(k):
        wires.arrived(n_row[k], rr.at[rows(k)], to_row)
        t2[rows(k), :] = total(own1[rows(k), :], rr[rows(k), :])
        wires.send(n_dp[k][0], t2.at[half(k, 1 - b)], rz.at[0, half(k, 1 - b)], to_dp[0])

    def from_dp(k, j):
        keep = half(k, b)
        wires.arrived(n_dp[k][j], rz.at[j, keep], to_dp[j])
        prior = t2[keep, :] if j == 0 else acc[j - 1, keep, :]
        value = total(prior, rz[j, keep, :])
        if j < bits - 1:
            acc[j, keep, :] = value
            wires.send(n_dp[k][j + 1], acc.at[j, keep], rz.at[j + 1, keep], to_dp[j + 1])
        else:
            res[keep, :] = value
            wires.send(n_back[k], res.at[keep], res.at[keep], to_dp[0])

    def pull_part():
        wires.arrived(n_dm, dm.at[1 - c], to_col)
        dm[c] = dmod[c]
        pull[0] = jnp.zeros((8, D), F32)
        for latent in range(2):
            low = dm[latent].astype(BF16)
            part = jnp.zeros((8, D), F32)
            for i in range(6):
                part += dot_nt(jnp.broadcast_to(low[i : i + 1, :], (8, HALF)), ada[:, i * HALF : (i + 1) * HALF])
            pull[0, latent : latent + 1, :] = part[:1]

    def pull_col():
        wires.send(n_p0, pull.at[0], pull.at[1], to_col)

    def pull_section():
        wires.arrived(n_p0, pull.at[1], to_col)
        pull[2] = pull[0] + pull[1]
        wires.send(n_p1, pull.at[2], pull.at[3], to_sec)

    me = 2 * z + r

    def fill_table():
        wires.arrived(n_p1, pull.at[3], to_sec)
        v = cond[...]
        sig = 1.0 / (1.0 + jnp.exp(-v))
        grad = (pull[2, 0:2, :] + pull[3, 0:2, :]) * (sig * (1.0 + v * (1.0 - sig)))
        cond_grad[...] = grad
        ids = [jnp.broadcast_to(ref[...].astype(F32), (2, D)) for ref in (labels, times)]
        mods = jnp.concatenate([dm[0, 0:6, :], dm[1, 0:6, :]], axis=1)
        table[me] = jnp.concatenate([grad, mods, silu[...], *ids, jnp.zeros((2, D), F32)], axis=0)

    def share_table(j):
        size = 1 << j
        block = pl.ds((me // size) * size, size)
        if j > 0:
            low = size // 2
            other = pl.ds(flipped(me // low, 1) * low, low)
            wires.arrived(n_table[j - 1], table.at[other], to_row if j == 1 else to_dp[j - 2])
        if j <= bits:
            wires.send(n_table[j], table.at[block], table.at[block], to_row if j == 0 else to_dp[j - 1])

    extra = [pull_part, pull_col, pull_section, fill_table]
    extra += [functools.partial(share_table, j) for j in range(bits + 2)]
    stages = [from_col, from_row] + [lambda k, j=j: from_dp(k, j) for j in range(bits)]
    for tick in range(max(count + len(stages), len(extra))):
        for stage, step in enumerate(stages):
            if 0 <= tick - stage < count:
                step(tick - stage)
        if tick < len(extra):
            extra[tick]()
    block_out[mine, :] = outs[c]
    input_grad[mine, :] = gin[c]
    wires.arrived(n_out, block_out.at[others], to_col)
    wires.arrived(n_gin, input_grad.at[others], to_col)
    for k in range(count):
        wires.arrived(n_back[k], res.at[half(k, 1 - b)], to_dp[0])
    g_qkv[:, :D] = res[:HALF, :].astype(F32)
    low = res[HALF:D, :].astype(F32)
    g_qkv[:, D:] = low[:, :HALF]
    g_proj[...] = low[:, HALF:]
    g_up[:, :D] = res[D : D + HALF, :].astype(F32)
    g_up[:, D:] = res[D + HALF : 2 * D, :].astype(F32)
    low = res[2 * D : 3 * D, :].astype(F32)
    g_down[:D, :] = low[:, :HALF]
    g_down[D:, :] = low[:, HALF:]
    tail[...] = res[ROWS:, :].astype(F32)
    wires.finish()


def remote_call(body, outs, scratch, args, wires, collective_id):
    vmem = pl.BlockSpec(memory_space=pltpu.VMEM)
    return pl.pallas_call(
        body,
        out_shape=[jax.ShapeDtypeStruct(s, d) for s, d in outs],
        in_specs=[vmem] * len(args),
        out_specs=[vmem] * len(outs),
        scratch_shapes=[pltpu.VMEM(s, d) for s, d in scratch]
        + [pltpu.SemaphoreType.DMA((wires,)), pltpu.SemaphoreType.DMA((wires,))],
        compiler_params=pltpu.CompilerParams(
            vmem_limit_bytes=60 * 1024 * 1024, collective_id=collective_id, has_side_effects=True
        ),
    )(*args)


def pack(qkv, proj, up, down):
    qkv = qkv.reshape(HALF, 3 * HALF)
    return jnp.concatenate(
        [
            qkv[:, :D],
            jnp.concatenate([qkv[:, D:], proj], axis=1),
            up[:, :D],
            up[:, D:],
            jnp.concatenate([down[:D], down[D:]], axis=1),
        ],
        axis=0,
    )


def on_device(
    latents_in,
    labels,
    timesteps,
    out_grad,
    label_table,
    time_table,
    ada_w,
    ada_b,
    qkv_w,
    qkv_b,
    proj_w,
    proj_b,
    fc1_w,
    fc1_b,
    fc2_w,
    fc2_b,
):
    section_zero = lax.axis_index("section") == 0
    own = latents_in.shape[0] // SEQ
    places = lax.axis_size("dp") * lax.axis_size("row")
    bits = lax.axis_size("dp").bit_length() - 1
    shard = pack(qkv_w[0], proj_w[0], fc1_w[0], fc2_w[0])
    ada_flat = ada_w[0].reshape(D, 6 * HALF)
    zero = jnp.zeros((HALF,), F32)
    bias = jnp.concatenate([qkv_b[0].reshape(3 * HALF), proj_b[0], fc1_b[0], fc2_b[0], zero]).reshape(5, D)
    bias = jnp.concatenate([bias, jnp.zeros((3, D), F32)], axis=0)
    labels2, times2 = labels[:, None], timesteps[:, None]
    shards, x, cot, mod, other_bias, silu, cond = remote_call(
        gather_kernel,
        [
            ((4, ROWS, D), BF16),
            ((SEQ, D), BF16),
            ((SEQ, D), BF16),
            ((8, D), F32),
            ((2, 8, D), F32),
            ((own, D), F32),
            ((own, D), F32),
        ],
        [((2, SEQ, HALF), BF16), ((2, SEQ, HALF), BF16), ((4, 8, HALF), F32), ((2, 8, D), F32)],
        (shard, latents_in, out_grad, labels2, times2, label_table, time_table, ada_flat, ada_b[0].reshape(1, 6 * HALF), bias),
        4 * PIECES + 6,
        0,
    )
    flat = bias.reshape(-1)
    col_flat, row_flat = other_bias[0].reshape(-1), other_bias[1].reshape(-1)
    row_one, col_one = lax.axis_index("row") == 1, lax.axis_index("col") == 1

    def ordered(is_second, other, at, size):
        mine, theirs = flat[at : at + size], other[at : at + size]
        return jnp.where(is_second, theirs, mine), jnp.where(is_second, mine, theirs)

    low, high = ordered(row_one, row_flat, 0, 3 * HALF)
    b_qkv = jnp.concatenate([low.reshape(3, HALF), high.reshape(3, HALF)], axis=1).reshape(1, 3 * D)
    b_proj = jnp.concatenate(ordered(col_one, col_flat, 3 * HALF, HALF)).reshape(1, D)
    b_up = jnp.concatenate(ordered(row_one, row_flat, 4 * HALF, FFH)).reshape(1, FF)
    b_down = jnp.concatenate(ordered(col_one, col_flat, 4 * HALF + FFH, HALF)).reshape(1, D)
    b = (b_qkv, b_proj, b_up, b_down)
    out1, *w = call(
        first_kernel,
        [((SEQ, D), BF16)] + [(s, BF16) for _, s in WEIGHTS],
        (x, mod, *b, shards),
    )
    received = lax.ppermute(out1, "section", [(0, 1)])
    x2 = jnp.where(section_zero, x, received)
    out, gin1, *saves = call(
        second_kernel,
        [((2, SEQ, HALF), BF16), ((SEQ, D), BF16)] + [(s, d) for _, s, d in SAVES],
        (x2, cot, mod, *b, *w),
    )
    grad_back = lax.ppermute(gin1, "section", [(1, 0)])
    cot2 = jnp.where(section_zero, grad_back, cot)
    gin, packed, dmod = call(
        third_kernel,
        [((2, SEQ, HALF), F32), ((4, GROWS, D), BF16), ((2, 8, HALF), F32)],
        (cot2, mod, *w, *saves),
    )
    vmem_half = ((GROWS, D), BF16)
    g_qkv, g_proj, g_up, g_down, tail, block_outs, input_grads, table, cond_grad = remote_call(
        functools.partial(reduce_kernel, bits),
        [
            ((HALF, 3 * HALF), F32),
            ((HALF, HALF), F32),
            ((HALF, FFH), F32),
            ((FFH, HALF), F32),
            ((GROWS - ROWS, D), F32),
            ((own * SEQ, HALF), BF16),
            ((own * SEQ, HALF), F32),
            ((places, 16, D), F32),
            ((own, D), F32),
        ],
        [
            ((2, GROWS, D), BF16),
            vmem_half,
            vmem_half,
            vmem_half,
            vmem_half,
            ((bits, GROWS, D), BF16),
            ((bits, GROWS, D), BF16),
            vmem_half,
            ((2, 8, HALF), F32),
            ((4, 8, D), F32),
        ],
        (packed, out, gin, dmod, cond, silu, labels2, times2, ada_flat),
        len(CHUNKS) * (4 + bits) + 5 + bits + 1,
        1,
    )
    grad_piece = table[:, 0:2].reshape(-1, D)
    dmod_piece = jnp.transpose(table[:, 2:8].reshape(places, 6, own, HALF), (0, 2, 1, 3)).reshape(-1, 6 * HALF)
    silu_piece = table[:, 8:10].reshape(-1, D).astype(BF16)
    label_ids = table[:, 10:12, 0].reshape(-1)
    step_ids = table[:, 12:14, 0].reshape(-1)
    ada_sum = dot_tn(silu_piece, dmod_piece.astype(BF16))
    adab_sum = jnp.sum(dmod_piece, axis=0)

    def table_sum(ids, count):
        hot = (ids[:, None] == jnp.arange(count, dtype=jnp.int32).astype(F32)[None, :]).astype(F32)
        return jnp.einsum("nc,na->ca", hot, grad_piece, precision=lax.Precision.HIGHEST)

    return (
        block_outs[None],
        input_grads[None],
        cond_grad,
        table_sum(label_ids, label_table.shape[0]),
        table_sum(step_ids, time_table.shape[0]),
        ada_sum.reshape(D, 6, HALF)[None],
        adab_sum.reshape(6, HALF)[None],
        g_qkv.reshape(HALF, 3, HALF)[None],
        jnp.concatenate([tail[0], tail[1, :HALF]]).reshape(3, HALF)[None],
        g_proj[None],
        tail[1, HALF:][None],
        g_up[None],
        jnp.concatenate([tail[2], tail[3]])[None],
        g_down[None],
        tail[4, :HALF][None],
    )


def solution(mesh):
    return jax.shard_map(
        on_device,
        mesh=mesh,
        in_specs=(
            P(("dp", "row"), "col"),
            P(("dp", "row")),
            P(("dp", "row")),
            P(("dp", "row"), "col"),
            P(),
            P(),
            P("section", None, None, "col"),
            P("section", None, "col"),
            P("section", "col", None, "row"),
            P("section", None, "row"),
            P("section", "row", "col"),
            P("section", "col"),
            P("section", "col", "row"),
            P("section", "row"),
            P("section", "row", "col"),
            P("section", "col"),
        ),
        out_specs=(
            P("section", ("dp", "row"), "col"),
            P("section", ("dp", "row"), "col"),
            P(("dp", "row"), None),
            P(),
            P(),
            P("section", None, None, "col"),
            P("section", None, "col"),
            P("section", "col", None, "row"),
            P("section", None, "row"),
            P("section", "row", "col"),
            P("section", "col"),
            P("section", "col", "row"),
            P("section", "row"),
            P("section", "row", "col"),
            P("section", "col"),
        ),
        check_vma=False,
    )
```

```python
import functools
import math

import jax
import jax.numpy as jnp
from jax import lax
from jax.experimental import pallas as pl
from jax.experimental.pallas import tpu as pltpu
from jax.sharding import PartitionSpec as P

D = 384
HALF = D // 2
HEADS = 6
HD = 64
FF = 1536
FFH = FF // 2
SEQ = 256
EPS = 1e-06
SCALE = 1.0 / math.sqrt(HD)
ROWS = 1152
GROWS = 1184
CHUNKS = ((0, 320), (320, 320), (640, 288), (928, 256))
MESH = pl.DeviceIdType.MESH
F32 = jnp.float32
BF16 = jnp.bfloat16


def dot(a, b):
    return jnp.dot(a, b, preferred_element_type=F32)


def dot_nt(a, b):
    return lax.dot_general(a, b, (((1,), (1,)), ((), ())), preferred_element_type=F32)


def dot_tn(a, b):
    return lax.dot_general(a, b, (((0,), (0,)), ((), ())), preferred_element_type=F32)


def shard_pieces(r, c):
    out = []
    for p, (pr, pc) in enumerate(((0, 0), (0, HALF), (HALF, 0))):
        out.append(("qkv", (c * HALF, HALF), (p * D + r * HALF, HALF), (pr, HALF), (pc, HALF)))
    out.append(("proj", (r * HALF, HALF), (c * HALF, HALF), (HALF, HALF), (HALF, HALF)))
    for k in range(2):
        out.append(("up", (c * HALF, HALF), (r * FFH + k * D, D), (D + k * HALF, HALF), (0, D)))
        out.append(("down", (r * FFH + k * D, D), (c * HALF, HALF), (2 * D, D), (k * HALF, HALF)))
    return out


def span(pair):
    return slice(pair[0], pair[0] + pair[1])


def norm_rows(v):
    mean_val = jnp.mean(v, axis=-1, keepdims=True)
    cen = v - mean_val
    inv = lax.rsqrt(jnp.mean(cen * cen, axis=-1, keepdims=True) + EPS)
    return cen * inv, inv


def norm_back(g, normed, inv):
    return inv * (
        g
        - jnp.mean(g, axis=-1, keepdims=True)
        - normed * jnp.mean(g * normed, axis=-1, keepdims=True)
    )


C0 = math.sqrt(2.0 / math.pi)


def gelu_parts(v):
    t = jnp.tanh(C0 * (v + 0.044715 * (v * v * v)))
    return 0.5 * v * (1.0 + t), t


def gelu_slope(v, t):
    return 0.5 * (1.0 + t) + 0.5 * v * (1.0 - t * t) * (C0 * (1.0 + 3.0 * 0.044715 * (v * v)))


def softmax(q, k):
    s = dot_nt(q, k) * SCALE
    e = jnp.exp(s - jnp.max(s, axis=-1, keepdims=True))
    return e * (1.0 / jnp.sum(e, axis=-1, keepdims=True))


def head(arr, part, h):
    at = part * D + h * HD
    return arr[:, at : at + HD]


def forward(x, mod, w, b, keep=None):
    def put(name, value):
        if keep is not None:
            keep[name][...] = value

    m = [mod[i : i + 1, :] for i in range(6)]
    normed1, inv1 = norm_rows(x)
    hidden1 = (normed1 * (1.0 + m[1]) + m[0]).astype(BF16)
    packed = (dot(hidden1, w["qkv"][...]) + b["qkv"]).astype(BF16)
    heads = []
    for h in range(HEADS):
        prob = softmax(head(packed, 0, h), head(packed, 1, h))
        heads.append(dot(prob.astype(BF16), head(packed, 2, h)).astype(BF16))
        if keep is not None:
            keep["prob"][h] = prob
    attended = jnp.concatenate(heads, axis=1)
    branch_a = dot(attended, w["proj"][...]) + b["proj"]
    middle = x + m[2] * branch_a
    normed2, inv2 = norm_rows(middle)
    hidden2 = (normed2 * (1.0 + m[4]) + m[3]).astype(BF16)
    pre = dot(hidden2, w["up"][...]) + b["up"]
    act, _ = gelu_parts(pre)
    act = act.astype(BF16)
    branch_f = dot(act, w["down"][...]) + b["down"]
    put("normed1", normed1)
    put("inv1", inv1)
    put("hidden1", hidden1)
    put("packed", packed)
    put("attended", attended)
    put("branch_a", branch_a)
    put("normed2", normed2)
    put("inv2", inv2)
    put("hidden2", hidden2)
    put("pre", pre)
    put("act", act)
    put("branch_f", branch_f)
    return (middle + m[5] * branch_f).astype(BF16)


SAVES = (
    ("normed1", (SEQ, D), F32),
    ("inv1", (SEQ, 1), F32),
    ("hidden1", (SEQ, D), BF16),
    ("packed", (SEQ, 3 * D), BF16),
    ("prob", (HEADS, SEQ, SEQ), F32),
    ("attended", (SEQ, D), BF16),
    ("branch_a", (SEQ, D), F32),
    ("normed2", (SEQ, D), F32),
    ("inv2", (SEQ, 1), F32),
    ("hidden2", (SEQ, D), BF16),
    ("pre", (SEQ, FF), F32),
    ("act", (SEQ, FF), BF16),
    ("branch_f", (SEQ, D), F32),
)
WEIGHTS = (("qkv", (D, 3 * D)), ("proj", (D, D)), ("up", (D, FF)), ("down", (FF, D)))


def col_sum(v):
    return jnp.sum(v.astype(F32), axis=0, keepdims=True)


def backward(grad_out, mod, w, s, put_w=None, put_b=None, dmod=None):
    full = put_w is not None
    m = [mod[i : i + 1, :] for i in range(6)]
    grad_f = (grad_out * m[5]).astype(BF16)
    pre = s["pre"][...]
    _, t = gelu_parts(pre)
    grad_pre = (dot_nt(grad_f, w["down"][...]) * gelu_slope(pre, t)).astype(BF16)
    if full:
        dmod[5] = col_sum(grad_out * s["branch_f"][...])
        put_w("down", dot_tn(s["act"][...], grad_f).astype(BF16))
        put_b("down", col_sum(grad_f))
    grad_h2 = dot_nt(grad_pre, w["up"][...])
    normed2 = s["normed2"][...]
    if full:
        put_w("up", dot_tn(s["hidden2"][...], grad_pre).astype(BF16))
        put_b("up", col_sum(grad_pre))
        dmod[4] = col_sum(grad_h2 * normed2)
        dmod[3] = col_sum(grad_h2)
    grad_mid = grad_out + norm_back(grad_h2 * (1.0 + m[4]), normed2, s["inv2"][...])
    grad_a = (grad_mid * m[2]).astype(BF16)
    if full:
        dmod[2] = col_sum(grad_mid * s["branch_a"][...])
        put_w("proj", dot_tn(s["attended"][...], grad_a).astype(BF16))
        put_b("proj", col_sum(grad_a))
    grad_att = dot_nt(grad_a, w["proj"][...]).astype(BF16)
    packed = s["packed"][...]
    parts = [[], [], []]
    for h in range(HEADS):
        q, k, v = (head(packed, i, h) for i in range(3))
        prob = s["prob"][h]
        g = grad_att[:, h * HD : (h + 1) * HD]
        grad_prob = dot_nt(g, v)
        delta = jnp.sum(prob * grad_prob, axis=-1, keepdims=True)
        gs = (prob * (grad_prob - delta) * SCALE).astype(BF16)
        parts[0].append(dot(gs, k).astype(BF16))
        parts[1].append(dot_tn(gs, q).astype(BF16))
        parts[2].append(dot_tn(prob.astype(BF16), g).astype(BF16))
    grad_packed = jnp.concatenate(parts[0] + parts[1] + parts[2], axis=1)
    normed1 = s["normed1"][...]
    grad_h1 = dot_nt(grad_packed, w["qkv"][...])
    if full:
        put_w("qkv", dot_tn(s["hidden1"][...], grad_packed).astype(BF16))
        put_b("qkv", col_sum(grad_packed))
        dmod[1] = col_sum(grad_h1 * normed1)
        dmod[0] = col_sum(grad_h1)
    return grad_mid + norm_back(grad_h1 * (1.0 + m[1]), normed1, s["inv1"][...])


def first_kernel(x_ref, mod_ref, bq, bp, bu, bd, shards, out_ref, wq, wp, wu, wd):
    w = dict(qkv=wq, proj=wp, up=wu, down=wd)
    for r in range(2):
        for c in range(2):
            for name, fr, fc, pr, pc in shard_pieces(r, c):
                w[name][span(fr), span(fc)] = shards[2 * r + c, span(pr), span(pc)]
    b = dict(qkv=bq[...], proj=bp[...], up=bu[...], down=bd[...])
    out_ref[...] = forward(x_ref[...].astype(F32), mod_ref, w, b)


def second_kernel(x_ref, g_ref, mod_ref, bq, bp, bu, bd, wq, wp, wu, wd, out_ref, gin_ref, *saves):
    w = dict(qkv=wq, proj=wp, up=wu, down=wd)
    s = {name: ref for (name, _, _), ref in zip(SAVES, saves)}
    b = dict(qkv=bq[...], proj=bp[...], up=bu[...], down=bd[...])
    out = forward(x_ref[...].astype(F32), mod_ref, w, b, s)
    for c in range(2):
        out_ref[c] = out[:, c * HALF : (c + 1) * HALF]
    gin_ref[...] = backward(g_ref[...].astype(F32), mod_ref, w, s).astype(BF16)


def third_kernel(g_ref, mod_ref, wq, wp, wu, wd, *rest):
    w = dict(qkv=wq, proj=wp, up=wu, down=wd)
    n = len(SAVES)
    s = {name: ref for (name, _, _), ref in zip(SAVES, rest[:n])}
    gin_ref, packed_ref, dmod_ref = rest[n:]
    packed_ref[:, ROWS:, :] = jnp.zeros((4, GROWS - ROWS, D), BF16)

    def put_w(name, value):
        for r in range(2):
            for c in range(2):
                for piece, fr, fc, pr, pc in shard_pieces(r, c):
                    if piece == name:
                        packed_ref[2 * r + c, span(pr), span(pc)] = value[span(fr), span(fc)]

    biases = {}
    put_b = biases.__setitem__
    dmod_ref[...] = jnp.zeros_like(dmod_ref)
    dmod = {}
    gin = backward(g_ref[...].astype(F32), mod_ref, w, s, put_w, put_b, dmod)
    for c in range(2):
        gin_ref[c] = gin[:, c * HALF : (c + 1) * HALF]
        for i in range(6):
            dmod_ref[c, i : i + 1, :] = dmod[i][:, c * HALF : (c + 1) * HALF]
    zero = jnp.zeros((1, HALF), F32)
    for r in range(2):
        for c in range(2):
            bq = [biases["qkv"][:, p * D + r * HALF : p * D + (r + 1) * HALF] for p in range(3)]
            rows = [
                jnp.concatenate(bq[:2], axis=1),
                jnp.concatenate([bq[2], biases["proj"][:, c * HALF : (c + 1) * HALF]], axis=1),
                biases["up"][:, r * FFH : r * FFH + D],
                biases["up"][:, r * FFH + D : (r + 1) * FFH],
                jnp.concatenate([biases["down"][:, c * HALF : (c + 1) * HALF], zero], axis=1),
                jnp.zeros((GROWS - ROWS - 5, D), F32),
            ]
            packed_ref[2 * r + c, ROWS:, :] = jnp.concatenate(rows, axis=0).astype(BF16)


def call(body, outs, args, flops=2_000_000_000):
    vmem = pl.BlockSpec(memory_space=pltpu.VMEM)
    return pl.pallas_call(
        body,
        out_shape=[jax.ShapeDtypeStruct(s, d) for s, d in outs],
        in_specs=[vmem] * len(args),
        out_specs=[vmem] * len(outs),
        compiler_params=pltpu.CompilerParams(vmem_limit_bytes=60 * 1024 * 1024),
        cost_estimate=pl.CostEstimate(flops=flops, bytes_accessed=8_000_000, transcendentals=800_000),
    )(*args)


def flipped(index, step):
    return index + step * (1 - 2 * lax.rem(index // step, 2))


def greet(partners):
    barrier = pltpu.get_barrier_semaphore()
    for where in partners:
        pl.semaphore_signal(barrier, inc=1, device_id=where, device_id_type=MESH)
    pl.semaphore_wait(barrier, len(partners))


class Wires:
    def __init__(self, send_sem, recv_sem):
        self.send_sem, self.recv_sem, self.started = send_sem, recv_sem, []

    def send(self, k, src, dst, where):
        copy = pltpu.make_async_remote_copy(
            src_ref=src,
            dst_ref=dst,
            send_sem=self.send_sem.at[k],
            recv_sem=self.recv_sem.at[k],
            device_id=where,
            device_id_type=MESH,
        )
        copy.start()
        self.started.append(copy)

    def arrived(self, k, dst, where):
        pltpu.make_async_remote_copy(
            src_ref=dst,
            dst_ref=dst,
            send_sem=self.send_sem.at[k],
            recv_sem=self.recv_sem.at[k],
            device_id=where,
            device_id_type=MESH,
        ).wait_recv()

    def finish(self):
        for copy in self.started:
            copy.wait_send()


PIECE = 192
PIECES = ROWS // 2 // PIECE


def gather_kernel(
    shard, lat, cot, labels, times, ltab, ttab, ada, adab, bias,
    out, x_out, cot_out, mod_out, bias_out, silu_out, cond_out,
    xr, cr, modbuf, biasbuf, send_sem, recv_sem,
):
    r, c, z = lax.axis_index("row"), lax.axis_index("col"), lax.axis_index("dp")
    h = lax.rem(z, 2)
    to_col, to_row, to_dp = {"col": 1 - c}, {"row": 1 - r}, {"dp": flipped(z, 1)}
    greet((to_col, to_row, to_dp))
    wires = Wires(send_sem, recv_sem)
    own, facing = 2 * r + c, 2 * (1 - r) + c

    def rows(half, i):
        return pl.ds(pl.multiple_of(half * (ROWS // 2) + i * PIECE, PIECE), PIECE)

    for i in range(PIECES):
        wires.send(i, shard.at[rows(h, i)], out.at[own, rows(h, i)], to_row)
    theirs = pl.ds(pl.multiple_of((1 - c) * SEQ, SEQ), SEQ)
    mine = pl.ds(pl.multiple_of(c * SEQ, SEQ), SEQ)
    base = 2 * PIECES
    wires.send(base, lat.at[theirs], xr.at[c], to_col)
    wires.send(base + 1, cot.at[theirs], cr.at[c], to_col)
    wires.send(base + 2, shard, out.at[own], to_col)
    wires.send(base + 3, bias, biasbuf.at[0], to_col)
    wires.send(base + 4, bias, biasbuf.at[1], to_row)
    out[own] = shard[...]
    xr[c] = lat[mine, :]
    cr[c] = cot[mine, :]

    def hot(ids, table):
        grid = lax.broadcasted_iota(jnp.int32, (ids.shape[0], table.shape[0]), 1)
        return dot(jnp.where(grid == ids[...], 1.0, 0.0).astype(BF16), table[...])

    cond = hot(labels, ltab) + hot(times, ttab)
    cond_out[...] = cond
    silu_low = (cond / (1.0 + jnp.exp(-cond))).astype(BF16)
    silu_out[...] = silu_low.astype(F32)
    modul = dot(silu_low, ada[...]) + adab[...]
    modbuf[0:2] = jnp.zeros((2, 8, HALF), F32)
    for latent in range(2):
        for i in range(6):
            modbuf[latent, i : i + 1, :] = modul[latent : latent + 1, i * HALF : (i + 1) * HALF]
    far = base + 6
    for i in range(PIECES):
        wires.arrived(i, out.at[facing, rows(h, i)], to_row)
        wires.send(PIECES + i, out.at[facing, rows(h, i)], out.at[facing, rows(h, i)], to_dp)
        wires.send(far + i, out.at[facing, rows(h, i)], out.at[facing, rows(h, i)], to_col)
        if i == 0:
            wires.send(base + 5, modbuf.at[1 - c], modbuf.at[2 + c], to_col)
    for i in range(PIECES):
        wires.arrived(PIECES + i, out.at[facing, rows(1 - h, i)], to_dp)
        wires.send(far + PIECES + i, out.at[facing, rows(1 - h, i)], out.at[facing, rows(1 - h, i)], to_col)
    wires.arrived(base, xr.at[1 - c], to_col)
    wires.arrived(base + 1, cr.at[1 - c], to_col)
    wires.arrived(base + 3, biasbuf.at[0], to_col)
    wires.arrived(base + 4, biasbuf.at[1], to_row)
    wires.arrived(base + 5, modbuf.at[2 + 1 - c], to_col)
    modbuf[2 + c] = modbuf[c]
    bias_out[...] = biasbuf[...]
    for half in range(2):
        x_out[:, half * HALF : (half + 1) * HALF] = xr[half]
        cot_out[:, half * HALF : (half + 1) * HALF] = cr[half]
        mod_out[:, half * HALF : (half + 1) * HALF] = modbuf[2 + half]
    wires.arrived(base + 2, out.at[2 * r + 1 - c], to_col)
    for i in range(PIECES):
        wires.arrived(far + i, out.at[2 * (1 - r) + 1 - c, rows(h, i)], to_col)
    for i in range(PIECES):
        wires.arrived(far + PIECES + i, out.at[2 * (1 - r) + 1 - c, rows(1 - h, i)], to_col)
    wires.finish()


def reduce_kernel(
    bits, packed, outs, gin, dmod, cond, silu, labels, times, ada,
    g_qkv, g_proj, g_up, g_down, tail, block_out, input_grad, table, cond_grad,
    rc, t1, own1, rr, t2, acc, rz, res, dm, pull, send_sem, recv_sem,
):
    r, c, z = lax.axis_index("row"), lax.axis_index("col"), lax.axis_index("dp")
    b = lax.rem(z, 2)
    sec = lax.axis_index("section")
    to_col, to_row, to_sec = {"col": 1 - c}, {"row": 1 - r}, {"section": 1 - sec}
    to_dp = [{"dp": flipped(z, 1 << j)} for j in range(bits)]
    greet((to_col, to_row, to_sec, *to_dp))
    wires = Wires(send_sem, recv_sem)
    count = len(CHUNKS)
    number = iter(range(1000))
    n_col = [[next(number) for _ in range(2)] for _ in CHUNKS]
    n_row = [next(number) for _ in CHUNKS]
    n_dp = [[next(number) for _ in range(bits)] for _ in CHUNKS]
    n_back = [next(number) for _ in CHUNKS]
    n_dm, n_p0, n_p1, n_out, n_gin = (next(number) for _ in range(5))
    n_table = [next(number) for _ in range(bits + 1)]

    def rows(k):
        return pl.ds(CHUNKS[k][0], CHUNKS[k][1])

    def half(k, which):
        size = CHUNKS[k][1] // 2
        return pl.ds(pl.multiple_of(CHUNKS[k][0] + which * size, 16), size)

    wires.send(n_dm, dmod.at[1 - c], dm.at[c], to_col)
    for k in range(count):
        for which, q in enumerate((1 - r, r)):
            wires.send(n_col[k][which], packed.at[2 * q + 1 - c, rows(k)], rc.at[q, rows(k)], to_col)
    mine = pl.ds(pl.multiple_of(c * SEQ, SEQ), SEQ)
    others = pl.ds(pl.multiple_of((1 - c) * SEQ, SEQ), SEQ)
    wires.send(n_out, outs.at[1 - c], block_out.at[mine], to_col)
    wires.send(n_gin, gin.at[1 - c], input_grad.at[mine], to_col)

    def total(left, right):
        return (left.astype(F32) + right.astype(F32)).astype(BF16)

    def from_col(k):
        wires.arrived(n_col[k][0], rc.at[1 - r, rows(k)], to_col)
        t1[rows(k), :] = total(packed[2 * (1 - r) + c, rows(k), :], rc[1 - r, rows(k), :])
        wires.send(n_row[k], t1.at[rows(k)], rr.at[rows(k)], to_row)
        wires.arrived(n_col[k][1], rc.at[r, rows(k)], to_col)
        own1[rows(k), :] = total(packed[2 * r + c, rows(k), :], rc[r, rows(k), :])

    def from_row(k):
        wires.arrived(n_row[k], rr.at[rows(k)], to_row)
        t2[rows(k), :] = total(own1[rows(k), :], rr[rows(k), :])
        wires.send(n_dp[k][0], t2.at[half(k, 1 - b)], rz.at[0, half(k, 1 - b)], to_dp[0])

    def from_dp(k, j):
        keep = half(k, b)
        wires.arrived(n_dp[k][j], rz.at[j, keep], to_dp[j])
        prior = t2[keep, :] if j == 0 else acc[j - 1, keep, :]
        value = total(prior, rz[j, keep, :])
        if j < bits - 1:
            acc[j, keep, :] = value
            wires.send(n_dp[k][j + 1], acc.at[j, keep], rz.at[j + 1, keep], to_dp[j + 1])
        else:
            res[keep, :] = value
            wires.send(n_back[k], res.at[keep], res.at[keep], to_dp[0])

    def pull_part():
        wires.arrived(n_dm, dm.at[1 - c], to_col)
        dm[c] = dmod[c]
        pull[0] = jnp.zeros((8, D), F32)
        for latent in range(2):
            low = dm[latent].astype(BF16)
            part = jnp.zeros((8, D), F32)
            for i in range(6):
                part += dot_nt(jnp.broadcast_to(low[i : i + 1, :], (8, HALF)), ada[:, i * HALF : (i + 1) * HALF])
            pull[0, latent : latent + 1, :] = part[:1]

    def pull_col():
        wires.send(n_p0, pull.at[0], pull.at[1], to_col)

    def pull_section():
        wires.arrived(n_p0, pull.at[1], to_col)
        pull[2] = pull[0] + pull[1]
        wires.send(n_p1, pull.at[2], pull.at[3], to_sec)

    me = 2 * z + r

    def fill_table():
        wires.arrived(n_p1, pull.at[3], to_sec)
        v = cond[...]
        sig = 1.0 / (1.0 + jnp.exp(-v))
        grad = (pull[2, 0:2, :] + pull[3, 0:2, :]) * (sig * (1.0 + v * (1.0 - sig)))
        cond_grad[...] = grad
        ids = [jnp.broadcast_to(ref[...].astype(F32), (2, D)) for ref in (labels, times)]
        mods = jnp.concatenate([dm[0, 0:6, :], dm[1, 0:6, :]], axis=1)
        table[me] = jnp.concatenate([grad, mods, silu[...], *ids, jnp.zeros((2, D), F32)], axis=0)

    def share_table(j):
        size = 1 << j
        block = pl.ds((me // size) * size, size)
        if j > 0:
            low = size // 2
            other = pl.ds(flipped(me // low, 1) * low, low)
            wires.arrived(n_table[j - 1], table.at[other], to_row if j == 1 else to_dp[j - 2])
        if j <= bits:
            wires.send(n_table[j], table.at[block], table.at[block], to_row if j == 0 else to_dp[j - 1])

    extra = [pull_part, pull_col, pull_section, fill_table]
    extra += [functools.partial(share_table, j) for j in range(bits + 2)]
    stages = [from_col, from_row] + [lambda k, j=j: from_dp(k, j) for j in range(bits)]
    for tick in range(max(count + len(stages), len(extra))):
        for stage, step in enumerate(stages):
            if 0 <= tick - stage < count:
                step(tick - stage)
        if tick < len(extra):
            extra[tick]()
    block_out[mine, :] = outs[c]
    input_grad[mine, :] = gin[c]
    wires.arrived(n_out, block_out.at[others], to_col)
    wires.arrived(n_gin, input_grad.at[others], to_col)
    for k in range(count):
        wires.arrived(n_back[k], res.at[half(k, 1 - b)], to_dp[0])
    g_qkv[:, :D] = res[:HALF, :].astype(F32)
    low = res[HALF:D, :].astype(F32)
    g_qkv[:, D:] = low[:, :HALF]
    g_proj[...] = low[:, HALF:]
    g_up[:, :D] = res[D : D + HALF, :].astype(F32)
    g_up[:, D:] = res[D + HALF : 2 * D, :].astype(F32)
    low = res[2 * D : 3 * D, :].astype(F32)
    g_down[:D, :] = low[:, :HALF]
    g_down[D:, :] = low[:, HALF:]
    tail[...] = res[ROWS:, :].astype(F32)
    wires.finish()


def remote_call(body, outs, scratch, args, wires, collective_id):
    vmem = pl.BlockSpec(memory_space=pltpu.VMEM)
    return pl.pallas_call(
        body,
        out_shape=[jax.ShapeDtypeStruct(s, d) for s, d in outs],
        in_specs=[vmem] * len(args),
        out_specs=[vmem] * len(outs),
        scratch_shapes=[pltpu.VMEM(s, d) for s, d in scratch]
        + [pltpu.SemaphoreType.DMA((wires,)), pltpu.SemaphoreType.DMA((wires,))],
        compiler_params=pltpu.CompilerParams(
            vmem_limit_bytes=60 * 1024 * 1024, collective_id=collective_id, has_side_effects=True
        ),
    )(*args)


def final_kernel(table, label_out, time_out, ada_out, adab_out):
    def hot_sum(at, count):
        total = jnp.zeros((count, D), F32)
        for l in range(2):
            ids = table[:, at + l, :][:, 0:1]
            grid = lax.broadcasted_iota(jnp.int32, (ids.shape[0], count), 1).astype(F32)
            total += lax.dot_general(
                jnp.where(grid == ids, 1.0, 0.0),
                table[:, l, :],
                (((0,), (0,)), ((), ())),
                preferred_element_type=F32,
                precision=lax.Precision.HIGHEST,
            )
        return total

    label_out[...] = hot_sum(10, label_out.shape[0])
    time_out[...] = hot_sum(12, time_out.shape[0])
    for i in range(6):
        mods = table[:, 2 + i, :]
        total = jnp.zeros((D, HALF), F32)
        for l in range(2):
            total += dot_tn(table[:, 8 + l, :].astype(BF16), mods[:, l * HALF : (l + 1) * HALF].astype(BF16))
        ada_out[:, i, :] = total
        sums = jnp.sum(mods, axis=0, keepdims=True)
        adab_out[i : i + 1, :] = sums[:, :HALF] + sums[:, HALF:]


def pack(qkv, proj, up, down):
    qkv = qkv.reshape(HALF, 3 * HALF)
    return jnp.concatenate(
        [
            qkv[:, :D],
            jnp.concatenate([qkv[:, D:], proj], axis=1),
            up[:, :D],
            up[:, D:],
            jnp.concatenate([down[:D], down[D:]], axis=1),
        ],
        axis=0,
    )


def on_device(
    latents_in,
    labels,
    timesteps,
    out_grad,
    label_table,
    time_table,
    ada_w,
    ada_b,
    qkv_w,
    qkv_b,
    proj_w,
    proj_b,
    fc1_w,
    fc1_b,
    fc2_w,
    fc2_b,
):
    section_zero = lax.axis_index("section") == 0
    own = latents_in.shape[0] // SEQ
    places = lax.axis_size("dp") * lax.axis_size("row")
    bits = lax.axis_size("dp").bit_length() - 1
    shard = pack(qkv_w[0], proj_w[0], fc1_w[0], fc2_w[0])
    ada_flat = ada_w[0].reshape(D, 6 * HALF)
    zero = jnp.zeros((HALF,), F32)
    bias = jnp.concatenate([qkv_b[0].reshape(3 * HALF), proj_b[0], fc1_b[0], fc2_b[0], zero]).reshape(5, D)
    bias = jnp.concatenate([bias, jnp.zeros((3, D), F32)], axis=0)
    labels2, times2 = labels[:, None], timesteps[:, None]
    shards, x, cot, mod, other_bias, silu, cond = remote_call(
        gather_kernel,
        [
            ((4, ROWS, D), BF16),
            ((SEQ, D), BF16),
            ((SEQ, D), BF16),
            ((8, D), F32),
            ((2, 8, D), F32),
            ((own, D), F32),
            ((own, D), F32),
        ],
        [((2, SEQ, HALF), BF16), ((2, SEQ, HALF), BF16), ((4, 8, HALF), F32), ((2, 8, D), F32)],
        (shard, latents_in, out_grad, labels2, times2, label_table, time_table, ada_flat, ada_b[0].reshape(1, 6 * HALF), bias),
        4 * PIECES + 6,
        0,
    )
    flat = bias.reshape(-1)
    col_flat, row_flat = other_bias[0].reshape(-1), other_bias[1].reshape(-1)
    row_one, col_one = lax.axis_index("row") == 1, lax.axis_index("col") == 1

    def ordered(is_second, other, at, size):
        mine, theirs = flat[at : at + size], other[at : at + size]
        return jnp.where(is_second, theirs, mine), jnp.where(is_second, mine, theirs)

    low, high = ordered(row_one, row_flat, 0, 3 * HALF)
    b_qkv = jnp.concatenate([low.reshape(3, HALF), high.reshape(3, HALF)], axis=1).reshape(1, 3 * D)
    b_proj = jnp.concatenate(ordered(col_one, col_flat, 3 * HALF, HALF)).reshape(1, D)
    b_up = jnp.concatenate(ordered(row_one, row_flat, 4 * HALF, FFH)).reshape(1, FF)
    b_down = jnp.concatenate(ordered(col_one, col_flat, 4 * HALF + FFH, HALF)).reshape(1, D)
    b = (b_qkv, b_proj, b_up, b_down)
    out1, *w = call(
        first_kernel,
        [((SEQ, D), BF16)] + [(s, BF16) for _, s in WEIGHTS],
        (x, mod, *b, shards),
    )
    received = lax.ppermute(out1, "section", [(0, 1)])
    x2 = jnp.where(section_zero, x, received)
    out, gin1, *saves = call(
        second_kernel,
        [((2, SEQ, HALF), BF16), ((SEQ, D), BF16)] + [(s, d) for _, s, d in SAVES],
        (x2, cot, mod, *b, *w),
    )
    grad_back = lax.ppermute(gin1, "section", [(1, 0)])
    cot2 = jnp.where(section_zero, grad_back, cot)
    gin, packed, dmod = call(
        third_kernel,
        [((2, SEQ, HALF), F32), ((4, GROWS, D), BF16), ((2, 8, HALF), F32)],
        (cot2, mod, *w, *saves),
    )
    vmem_half = ((GROWS, D), BF16)
    g_qkv, g_proj, g_up, g_down, tail, block_outs, input_grads, table, cond_grad = remote_call(
        functools.partial(reduce_kernel, bits),
        [
            ((HALF, 3 * HALF), F32),
            ((HALF, HALF), F32),
            ((HALF, FFH), F32),
            ((FFH, HALF), F32),
            ((GROWS - ROWS, D), F32),
            ((own * SEQ, HALF), BF16),
            ((own * SEQ, HALF), F32),
            ((places, 16, D), F32),
            ((own, D), F32),
        ],
        [
            ((2, GROWS, D), BF16),
            vmem_half,
            vmem_half,
            vmem_half,
            vmem_half,
            ((bits, GROWS, D), BF16),
            ((bits, GROWS, D), BF16),
            vmem_half,
            ((2, 8, HALF), F32),
            ((4, 8, D), F32),
        ],
        (packed, out, gin, dmod, cond, silu, labels2, times2, ada_flat),
        len(CHUNKS) * (4 + bits) + 5 + bits + 1,
        1,
    )
    label_sum, time_sum, ada_sum, adab_sum = call(
        final_kernel,
        [(label_table.shape, F32), (time_table.shape, F32), ((D, 6, HALF), F32), ((6, HALF), F32)],
        (table,),
    )
    return (
        block_outs[None],
        input_grads[None],
        cond_grad,
        label_sum,
        time_sum,
        ada_sum[None],
        adab_sum[None],
        g_qkv.reshape(HALF, 3, HALF)[None],
        jnp.concatenate([tail[0], tail[1, :HALF]]).reshape(3, HALF)[None],
        g_proj[None],
        tail[1, HALF:][None],
        g_up[None],
        jnp.concatenate([tail[2], tail[3]])[None],
        g_down[None],
        tail[4, :HALF][None],
    )


def solution(mesh):
    return jax.shard_map(
        on_device,
        mesh=mesh,
        in_specs=(
            P(("dp", "row"), "col"),
            P(("dp", "row")),
            P(("dp", "row")),
            P(("dp", "row"), "col"),
            P(),
            P(),
            P("section", None, None, "col"),
            P("section", None, "col"),
            P("section", "col", None, "row"),
            P("section", None, "row"),
            P("section", "row", "col"),
            P("section", "col"),
            P("section", "col", "row"),
            P("section", "row"),
            P("section", "row", "col"),
            P("section", "col"),
        ),
        out_specs=(
            P("section", ("dp", "row"), "col"),
            P("section", ("dp", "row"), "col"),
            P(("dp", "row"), None),
            P(),
            P(),
            P("section", None, None, "col"),
            P("section", None, "col"),
            P("section", "col", None, "row"),
            P("section", None, "row"),
            P("section", "row", "col"),
            P("section", "col"),
            P("section", "col", "row"),
            P("section", "row"),
            P("section", "row", "col"),
            P("section", "col"),
        ),
        check_vma=False,
    )
```
